32 devices in a mesh: dp: 4 (over z), cp: 8 (over y, x, core).
Axes of the slice: x: 2, y: 2, z: 4, core: 2. Of those that a mesh axis runs over, the one named last changes fastest.
Arguments:
- row_owner: int32 [4096, 1], P(('dp', 'cp')), may hold values from 0 to 31; in each aligned block of 128 rows (0 to 127, 128 to 255, ...) at most 10 rows name the same one
- slot_row: int32 [4096], P(('dp', 'cp')), may hold values from 0 to 2559
- hot_table: bfloat16 [16384, 512], P(('dp', 'cp')), may hold values from -6 to 6
- cold_table: bfloat16 [65536, 128], P(('dp', 'cp')), may hold values from -6 to 6
- cold_projection: bfloat16 [128, 512], replicated, may hold values from -0.5 to 0.5
- joined_weight: bfloat16 [512, 2048], replicated, may hold values from -0.25 to 0.25
- output_weight: bfloat16 [512, 512], replicated, may hold values from -0.25 to 0.25
- cotangent: bfloat16 [4096, 512], P(('dp', 'cp')), may hold values from -6 to 6
Outputs:
- layer_out: bfloat16 [4096, 512], P(('dp', 'cp'))
- hot_gradient: float32 [16384, 512], P(('dp', 'cp'))
- cold_gradient: float32 [65536, 128], P(('dp', 'cp'))
- projection_gradient: float32 [128, 512], replicated
- joined_gradient: float32 [512, 2048], replicated
- output_gradient: float32 [512, 512], replicated
The draws below stay inside these ranges and needn't reach their ends.
Inputs may be any that keep to these rules, and one draw needn't show every extreme that they name: `row_owner`: in each aligned block of 128 rows (the rows of one device) no owner is named by more than 10 rows.
All inputs are finite; a program needn't handle non-finite values.
Results may differ from the reference program's by a relative error of at most 0.013.
Values may be sent and summed in bfloat16 or wider, within the bound.
No kernel may reach another device: no remote copies, remote signals or barrier semaphores. Data moves between devices by JAX's collectives and lax.ppermute only.
A program may use at most 128 MiB of HBM per device.

```python
import math
import jax
import jax.numpy as jnp
import numpy as np
from jax import lax

D = 512
HEADS = 8
HEAD = 64
COLD_W = 128
TOK_DEV = 128
HOT_DEV = 512
COLD_DEV = 2048
LENGTH = 1024
TOKENS = 4096
CAP = 10
HOT_ALL = 16384
COLD_ALL = 65536
N_DP = 4
DEVICES = 32


def touch_ends(values, rng, least, top_value):
    longest = values.shape.index(max(values.shape))
    spots = []
    for shift in (0, 1):
        where = [jax.random.randint(jax.random.fold_in(rng, axis), (), 0, length) for axis, length in enumerate(values.shape)]
        where[longest] = (where[longest] + shift) % values.shape[longest]
        spots.append(tuple(where))
    return values.at[spots[0]].set(least).at[spots[1]].set(top_value)


def steps_of(own_key, extent, pieces, low, high):
    def one(axis_at, parts):
        draws = jax.random.uniform(jax.random.fold_in(jax.random.fold_in(own_key, 6), axis_at), (parts,), jnp.float32, low / len(pieces), high / len(pieces))
        return jnp.repeat(jnp.exp(draws), extent[axis_at] // parts).reshape((-1,) + (1,) * (len(extent) - axis_at - 1))

    gain = one(*pieces[0])
    for cut in pieces[1:]:
        gain = gain * one(*cut)
    return gain


def deal_out(stream_key, own, number, rows, amount, top, bound, skew):
    ranking = jax.random.permutation(stream_key, amount)
    heavy_load, common = shares(amount, rows * top, bound, skew, True), shares(amount, rows * top, bound, skew, False)
    places = jnp.arange(amount)

    def named(tallies, rotation):
        used = int((tallies > 0).sum())
        fixed = max(1, used // 4)
        passed = fixed + (places - fixed + rotation * (used - fixed)) % max(1, amount - fixed)
        return jnp.zeros((amount,), jnp.int32).at[ranking[jnp.where(places < fixed, places, passed)]].set(jnp.asarray(tallies, jnp.int32))

    tallies = jnp.where(number % 4 == 0, named(heavy_load, number // 4), named(common, number - number // 4 - 1))
    mixed = jax.random.permutation(jax.random.fold_in(own, 3), amount)
    donor, receiver = mixed[0:amount // 2 * 2:2], mixed[1:amount // 2 * 2:2]
    room = jnp.minimum(tallies[donor] - 1, bound - tallies[receiver]) // 2
    room = jnp.where((donor == ranking[0]) | (receiver == ranking[0]) | (tallies[receiver] == 0), 0, jnp.maximum(room, 0))
    passed = jax.random.randint(jax.random.fold_in(own, 4), (amount // 2,), 0, 1 << 20) % (room + 1)
    tallies = tallies.at[donor].add(-passed).at[receiver].add(passed)
    labels = jnp.searchsorted(jnp.cumsum(tallies), jnp.arange(rows * top), side="right").astype(jnp.int32)
    listing = labels.reshape(top, rows).T
    listing = listing[jax.random.permutation(jax.random.fold_in(own, 1), rows)]
    rotation = jax.random.randint(jax.random.fold_in(own, 2), (rows, 1), 0, top)
    return jnp.take_along_axis(listing, (jnp.arange(top)[None, :] + rotation) % top, axis=1)


def shares(count, total, bound, lean, full):
    portions = [(1 << 20) // math.isqrt(rank ** lean) + 1 for rank in range(1, count + 1)]
    largest = bound if full else min(bound, max(-(-total // count), total * portions[0] // sum(portions)))
    least = 1 if total - largest >= count - 1 else 0
    holding, spare = [largest] + [least] * (count - 1), total - largest - least * (count - 1)
    while spare > 0:
        free = [i for i in range(1, count) if holding[i] < largest] or [i for i in range(1, count) if holding[i] < bound]
        whole, remaining = sum([portions[i] for i in free]), spare
        for i in free:
            more = min(bound - holding[i], max(1, remaining * portions[i] // whole), spare)
            holding[i] = holding[i] + more
            spare = spare - more
    return np.array(holding)


def normal_values(stream_key, dims, width, bound, split=(), kind=jnp.bfloat16):
    values = width * jax.random.normal(stream_key, dims, jnp.float32)
    if split:
        values = values * steps_of(stream_key, dims, split, -0.22, 0.18)
    return jnp.clip(values, -bound, bound).astype(kind)


def setup_inputs(seed: int = 0) -> dict:
    key_list = jax.random.split(jax.random.key(seed), 9)
    row_owner_keys = jax.random.split(jax.random.fold_in(key_list[0], 1), TOKENS // TOK_DEV)
    row_owner_turns = jax.random.permutation(jax.random.fold_in(key_list[0], 3), TOKENS // TOK_DEV)
    row_owner = jax.vmap(lambda own, number: deal_out(jax.random.fold_in(key_list[0], 2), own, number, TOK_DEV, DEVICES, 1, CAP, 2))(row_owner_keys, row_owner_turns).reshape((TOKENS, 1))
    slot_row = touch_ends(jax.random.randint(key_list[1], (TOKENS,), 0, HOT_DEV + COLD_DEV), jax.random.fold_in(key_list[1], 1), 0, (HOT_DEV + COLD_DEV) - 1).astype(jnp.int32)
    hot_table = normal_values(key_list[2], (HOT_ALL, D), 1.0, 6.0, ((0, 32),))
    cold_table = normal_values(key_list[3], (COLD_ALL, COLD_W), 1.0, 6.0, ((0, 32),))
    cold_projection = normal_values(key_list[4], (COLD_W, D), COLD_W ** -0.5, 0.5)
    joined_weight = normal_values(key_list[5], (D, 4 * D), D ** -0.5, 0.25)
    output_weight = normal_values(key_list[6], (D, D), D ** -0.5, 0.25)
    cotangent = normal_values(key_list[7], (TOKENS, D), 1.0, 6.0, ((0, 32),))
    return {"row_owner": row_owner, "slot_row": slot_row, "hot_table": hot_table, "cold_table": cold_table, "cold_projection": cold_projection, "joined_weight": joined_weight, "output_weight": output_weight, "cotangent": cotangent}


EPSILON = 1e-05

def silu_slope(values):
    sigmoid_v = jax.nn.sigmoid(values)
    return sigmoid_v * (1.0 + values * (1.0 - sigmoid_v))

def layer_normalize(values):
    average = lax.optimization_barrier(jnp.mean(values, axis=-1, keepdims=True))
    centred = values - average
    inverse = lax.rsqrt(lax.optimization_barrier(jnp.mean(centred * centred, axis=-1, keepdims=True)) + EPSILON)
    return (centred * inverse, inverse)

def normalize_back(gradient, normed, inverse):
    first_term = lax.optimization_barrier(jnp.mean(gradient, axis=-1, keepdims=True))
    second_term = lax.optimization_barrier(jnp.mean(gradient * normed, axis=-1, keepdims=True))
    return (gradient - first_term - normed * second_term) * inverse

def rounded_float(values):
    return lax.optimization_barrier(values.astype(jnp.bfloat16)).astype(jnp.float32)

def sequence_forward(query_heads, key_heads, value_heads):
    block_rows = min(LENGTH, 512)
    score_scale = 1.0 / math.sqrt(HEAD)
    key_index = jnp.arange(LENGTH, dtype=jnp.int32)
    key_float = key_heads.astype(jnp.float32)
    value_float = value_heads.astype(jnp.float32)

    def one_block(counter):
        offset = counter * block_rows
        query_block = lax.dynamic_slice_in_dim(query_heads, offset, block_rows, 0).astype(jnp.float32)
        scores = jnp.einsum('qhd,khd->hqk', query_block, key_float) * score_scale
        query_index = offset + jnp.arange(block_rows, dtype=jnp.int32)
        allowed = (key_index[None, :] <= query_index[:, None])[None]
        weights = rounded_float(jnp.where(allowed, jax.nn.silu(scores), 0.0))
        return jnp.einsum('hqk,khd->qhd', weights, value_float)
    result = lax.map(one_block, jnp.arange(LENGTH // block_rows, dtype=jnp.int32))
    return result.reshape(LENGTH, HEADS * HEAD)

def sequence_backward(query_heads, key_heads, value_heads, delta_heads):
    block_rows = min(LENGTH, 512)
    score_scale = 1.0 / math.sqrt(HEAD)
    key_index = jnp.arange(LENGTH, dtype=jnp.int32)
    key_float = key_heads.astype(jnp.float32)
    value_float = value_heads.astype(jnp.float32)

    def one_block(carried, counter):
        key_sum, value_sum = carried
        offset = counter * block_rows
        query_block = lax.dynamic_slice_in_dim(query_heads, offset, block_rows, 0).astype(jnp.float32)
        delta_block = lax.dynamic_slice_in_dim(delta_heads, offset, block_rows, 0).astype(jnp.float32)
        scores = jnp.einsum('qhd,khd->hqk', query_block, key_float) * score_scale
        query_index = offset + jnp.arange(block_rows, dtype=jnp.int32)
        allowed = (key_index[None, :] <= query_index[:, None])[None]
        weights = rounded_float(jnp.where(allowed, jax.nn.silu(scores), 0.0))
        delta_weights = jnp.einsum('qhd,khd->hqk', delta_block, value_float)
        delta_scores = rounded_float(jnp.where(allowed, delta_weights * silu_slope(scores) * score_scale, 0.0))
        query_part = jnp.einsum('hqk,khd->qhd', delta_scores, key_float)
        key_sum = key_sum + jnp.einsum('hqk,qhd->khd', delta_scores, query_block)
        value_sum = value_sum + jnp.einsum('hqk,qhd->khd', weights, delta_block)
        return ((key_sum, value_sum), query_part)
    empty_heads = jnp.zeros((LENGTH, HEADS, HEAD), jnp.float32)
    (key_sum, value_sum), query_parts = lax.scan(one_block, (empty_heads, empty_heads), jnp.arange(LENGTH // block_rows, dtype=jnp.int32))
    return (query_parts.reshape(LENGTH, HEADS * HEAD), key_sum.reshape(LENGTH, HEADS * HEAD), value_sum.reshape(LENGTH, HEADS * HEAD))

def reference(row_owner, slot_row, hot_table, cold_table, cold_projection, joined_weight, output_weight, cotangent):
    owners = row_owner[:, 0]
    is_hot = slot_row < HOT_DEV
    is_cold = jnp.logical_not(is_hot)
    hot_index = jnp.where(is_hot, owners * HOT_DEV + slot_row, 0).astype(jnp.int32)
    cold_index = jnp.where(is_hot, 0, owners * COLD_DEV + slot_row - HOT_DEV).astype(jnp.int32)
    hot_rows = hot_table[hot_index]
    cold_rows = cold_table[cold_index]
    cold_embed = jnp.dot(cold_rows, cold_projection, preferred_element_type=jnp.float32)
    embedded = jnp.where(is_hot[:, None], hot_rows.astype(jnp.float32), cold_embed)
    normed, inverse = layer_normalize(embedded)
    normed_low = normed.astype(jnp.bfloat16)
    hidden = jnp.dot(normed_low, joined_weight, preferred_element_type=jnp.float32)
    active = jax.nn.silu(hidden).astype(jnp.bfloat16)
    gate_part = active[:, :D]
    shaped = active[:, D:].reshape(N_DP, LENGTH, 3, HEADS, HEAD)
    value_rows = shaped[:, :, 0]
    query_rows = shaped[:, :, 1]
    key_rows = shaped[:, :, 2]
    attended = lax.map(lambda items: sequence_forward(*items), (query_rows, key_rows, value_rows)).reshape(TOKENS, D)
    mixed, inverse_mix = layer_normalize(attended)
    gated = (mixed * gate_part.astype(jnp.float32)).astype(jnp.bfloat16)
    branch = jnp.dot(gated, output_weight, preferred_element_type=jnp.float32)
    layer_out = (embedded + branch).astype(jnp.bfloat16)
    delta_gated = jnp.dot(cotangent, output_weight.T, preferred_element_type=jnp.float32)
    delta_gate = delta_gated * mixed
    delta_attended = normalize_back(delta_gated * gate_part.astype(jnp.float32), mixed, inverse_mix).astype(jnp.bfloat16)
    delta_heads = delta_attended.reshape(N_DP, LENGTH, HEADS, HEAD)
    delta_query, delta_key, delta_value = lax.map(lambda items: sequence_backward(*items), (query_rows, key_rows, value_rows, delta_heads))
    delta_active = jnp.concatenate([delta_gate, delta_value.reshape(TOKENS, D), delta_query.reshape(TOKENS, D), delta_key.reshape(TOKENS, D)], axis=1)
    delta_hidden = (delta_active * silu_slope(hidden)).astype(jnp.bfloat16)
    delta_normed = jnp.dot(delta_hidden, joined_weight.T, preferred_element_type=jnp.float32)
    delta_embed = normalize_back(delta_normed, normed, inverse) + cotangent.astype(jnp.float32)
    hot_gradient = jnp.zeros((HOT_ALL, D), jnp.float32).at[hot_index].add(jnp.where(is_hot[:, None], delta_embed, 0.0))
    cold_event = jnp.dot(delta_embed, cold_projection.astype(jnp.float32).T, precision=lax.Precision.HIGHEST)
    cold_gradient = jnp.zeros((COLD_ALL, COLD_W), jnp.float32).at[cold_index].add(jnp.where(is_cold[:, None], cold_event, 0.0))
    norm_scale = TOKENS ** (-0.5)
    cold_float = jnp.where(is_cold[:, None], cold_rows.astype(jnp.float32), 0.0)
    projection_gradient = jnp.dot(cold_float.T, delta_embed, precision=lax.Precision.HIGHEST) * norm_scale
    joined_gradient = jnp.dot(normed_low.T, delta_hidden, preferred_element_type=jnp.float32) * norm_scale
    output_gradient = jnp.dot(gated.T, cotangent, preferred_element_type=jnp.float32) * norm_scale
    return (layer_out, hot_gradient, cold_gradient, projection_gradient, joined_gradient, output_gradient)
```

```python
import math

import jax
import jax.numpy as jnp
from jax import lax
from jax.sharding import PartitionSpec as P

HEADS = 8


EPSILON = 1e-05


def silu_slope(values):
    sigmoid_v = jax.nn.sigmoid(values)
    return sigmoid_v * (1.0 + values * (1.0 - sigmoid_v))


def layer_normalize(values):
    average = jnp.mean(values, axis=-1, keepdims=True)
    centred = values - average
    inverse = lax.rsqrt(jnp.mean(centred * centred, axis=-1, keepdims=True) + EPSILON)
    return (centred * inverse, inverse)


def normalize_back(gradient, normed, inverse):
    first_term = jnp.mean(gradient, axis=-1, keepdims=True)
    second_term = jnp.mean(gradient * normed, axis=-1, keepdims=True)
    return (gradient - first_term - normed * second_term) * inverse


def exchange(block, axis, step):
    count = lax.axis_size(axis)
    if count & (count - 1) == 0:
        pairs = [(i, i ^ step) for i in range(count)]
        source = lax.axis_index(axis) ^ step
        target = source
    else:
        pairs = [(i, (i + step) % count) for i in range(count)]
        source = (lax.axis_index(axis) - step) % count
        target = (lax.axis_index(axis) + step) % count
    if callable(block):
        block = block(target)
    return lax.ppermute(block, axis, pairs), source


def gather_blocks(block, axis):
    count = lax.axis_size(axis)
    here = lax.axis_index(axis)
    result = jnp.zeros((count,) + block.shape, block.dtype)
    if count & (count - 1) or count < 4:
        pieces = [(block, here)] + [exchange(block, axis, step) for step in range(1, count)]
        for piece, source in pieces:
            result = lax.dynamic_update_index_in_dim(result, piece, source, 0)
        return result
    pieces = [(block, here)] + [exchange(block, axis, step) for step in range(2, count, 2)]
    stack = jnp.stack([piece for piece, source in pieces])
    other, source = exchange(stack, axis, 1)
    for at, (piece, source) in enumerate(pieces):
        result = lax.dynamic_update_index_in_dim(result, piece, source, 0)
        result = lax.dynamic_update_index_in_dim(result, other[at], source ^ 1, 0)
    return result


def reduce_blocks(partial, axis):
    count = lax.axis_size(axis)
    low = partial.astype(jnp.bfloat16).reshape((count, -1, partial.shape[-1]))
    total = lax.dynamic_index_in_dim(
        partial.reshape(low.shape), lax.axis_index(axis), 0, keepdims=False
    )

    def chunk(target):
        return lax.dynamic_index_in_dim(low, target, 0, keepdims=False)

    for step in range(1, count):
        arrived, source = exchange(chunk, axis, step)
        total = total + arrived.astype(jnp.float32)
    return total


def reduce_gather(partial):
    mine = reduce_blocks(partial, "dp").astype(jnp.bfloat16)
    row = gather_blocks(mine, "dp").reshape(partial.shape)
    return gather_blocks(row, "cp")


def to_columns(rows, axis):
    count = lax.axis_size(axis)
    tokens, parts, width = rows.shape
    split = rows.reshape(tokens, parts, count, width // count)
    split = split.transpose(2, 0, 1, 3).reshape(count, tokens, parts * width // count)
    moved = lax.all_to_all(split, axis, split_axis=0, concat_axis=0, tiled=True)
    return moved.reshape(count * tokens, parts * width // count)


def local(
    row_owner,
    slot_row,
    hot_table,
    cold_table,
    cold_projection,
    joined_weight,
    output_weight,
    cotangent,
):
    tokens = slot_row.shape[0]
    width = output_weight.shape[0]
    hot_count = hot_table.shape[0]
    cold_count, cold_width = cold_table.shape
    head_size = width // HEADS
    score_scale = 1.0 / math.sqrt(head_size)
    everyone = ("dp", "cp")
    devices = lax.axis_size(everyone)
    group = lax.axis_size("cp")
    here = lax.axis_index("cp")
    length = group * tokens
    capacity = 2 * tokens // devices + 2
    low = jnp.bfloat16
    f32 = jnp.float32
    owners = row_owner[:, 0]
    is_hot = slot_row < hot_count
    is_cold = jnp.logical_not(is_hot)
    named = owners[:, None] == jnp.arange(devices, dtype=jnp.int32)[None, :]
    onehot = named.astype(low)
    lower = (jnp.arange(tokens)[:, None] > jnp.arange(tokens)[None, :]).astype(low)
    earlier = jnp.dot(lower, onehot, preferred_element_type=f32)
    rank = jnp.sum(jnp.where(named, earlier, 0.0), axis=1).astype(jnp.int32)
    place = owners * capacity + rank
    places = jnp.arange(devices * capacity, dtype=jnp.int32)
    chosen = place[:, None] == places[None, :]
    requests = jnp.max(jnp.where(chosen, slot_row[:, None], -1), axis=0)
    asked = lax.all_to_all(
        requests.reshape(devices, capacity), everyone, split_axis=0, concat_axis=0, tiled=True
    ).reshape(-1)
    hot_select = asked[:, None] == jnp.arange(hot_count, dtype=jnp.int32)[None, :]
    cold_select = asked[:, None] == jnp.arange(hot_count, hot_count + cold_count, dtype=jnp.int32)
    hot_pick = jnp.dot(hot_select.astype(low), hot_table, preferred_element_type=low)
    cold_pick = jnp.dot(cold_select.astype(low), cold_table, preferred_element_type=low)
    picked = hot_pick + jnp.pad(cold_pick, ((0, 0), (0, width - cold_width)))
    rows_back = lax.all_to_all(
        picked.reshape(devices, capacity, width), everyone, split_axis=0, concat_axis=0, tiled=True
    ).reshape(devices * capacity, width)
    vector = jnp.dot(chosen.astype(low), rows_back, preferred_element_type=low)
    cold_vector = vector[:, :cold_width]
    cold_embed = jnp.dot(cold_vector, cold_projection, preferred_element_type=f32)
    embedded = jnp.where(is_hot[:, None], vector.astype(f32), cold_embed)
    normed, inverse = layer_normalize(embedded)
    normed_low = normed.astype(low)
    all_cotangent = gather_blocks(cotangent, "cp").reshape(length, width)
    all_normed = gather_blocks(normed_low, "cp").reshape(length, width)
    hidden = jnp.dot(normed_low, joined_weight, preferred_element_type=f32)
    slope = silu_slope(hidden)
    active = jax.nn.silu(hidden).astype(low)
    gate = active[:, :width].astype(f32)
    all_hidden = jnp.dot(all_normed, joined_weight[:, width:], preferred_element_type=f32)
    all_active = jax.nn.silu(all_hidden).astype(low)

    def heads_of(rows):
        return rows.reshape(rows.shape[0], HEADS, head_size)

    values, queries, keys = (heads_of(active[:, n * width : (n + 1) * width]) for n in (1, 2, 3))
    all_values, all_queries, all_keys = (
        heads_of(all_active[:, n * width : (n + 1) * width]) for n in (0, 1, 2)
    )
    own_index = here * tokens + jnp.arange(tokens, dtype=jnp.int32)
    all_index = jnp.arange(length, dtype=jnp.int32)
    scores = jnp.einsum("qhd,khd->hqk", queries, all_keys, preferred_element_type=f32)
    scores = scores * score_scale
    allowed = (all_index[None, :] <= own_index[:, None])[None]
    weights = jnp.where(allowed, jax.nn.silu(scores), 0.0).astype(low)
    attended = jnp.einsum("hqk,khd->qhd", weights, all_values, preferred_element_type=f32)
    attended = attended.reshape(tokens, width)
    mixed, inverse_mix = layer_normalize(attended)
    gated = (mixed * gate).astype(low)
    branch = jnp.dot(gated, output_weight, preferred_element_type=f32)
    layer_out = (embedded + branch).astype(low)
    delta_gated = jnp.dot(cotangent, output_weight.T, preferred_element_type=f32)
    delta_gate = delta_gated * mixed
    delta_attended = normalize_back(delta_gated * gate, mixed, inverse_mix).astype(low)
    all_delta = heads_of(gather_blocks(delta_attended, "cp").reshape(length, width))
    delta = heads_of(delta_attended)
    gate_hidden = (delta_gate * slope[:, :width]).astype(low)
    early = to_columns(jnp.stack([gated, gate_hidden], axis=1), "cp")
    share = width // group
    out_part = jnp.dot(early[:, :share].T, all_cotangent, preferred_element_type=f32)
    gate_part = jnp.dot(early[:, share:].T, all_normed, preferred_element_type=f32)
    first = reduce_gather(jnp.concatenate([out_part, gate_part], axis=0))

    delta_weights = jnp.einsum("qhd,khd->hqk", delta, all_values, preferred_element_type=f32)
    delta_scores = jnp.where(
        allowed, delta_weights * silu_slope(scores) * score_scale, 0.0
    ).astype(low)
    delta_query = jnp.einsum("hqk,khd->qhd", delta_scores, all_keys, preferred_element_type=f32)
    later = (own_index[:, None] <= all_index[None, :])[None]
    turned = jnp.einsum("khd,qhd->hkq", keys, all_queries, preferred_element_type=f32)
    turned = turned * score_scale
    turned_weights = jnp.where(later, jax.nn.silu(turned), 0.0).astype(low)
    turned_delta = jnp.einsum("khd,qhd->hkq", values, all_delta, preferred_element_type=f32)
    turned_scores = jnp.where(
        later, turned_delta * silu_slope(turned) * score_scale, 0.0
    ).astype(low)
    delta_value = jnp.einsum("hkq,qhd->khd", turned_weights, all_delta, preferred_element_type=f32)
    delta_key = jnp.einsum("hkq,qhd->khd", turned_scores, all_queries, preferred_element_type=f32)
    rest = jnp.concatenate(
        [part.reshape(tokens, width) for part in (delta_value, delta_query, delta_key)], axis=1
    )
    rest_hidden = (rest * slope[:, width:]).astype(low)
    late = to_columns(rest_hidden.reshape(tokens, 3, width), "cp")
    second = reduce_gather(jnp.dot(late.T, all_normed, preferred_element_type=f32))
    delta_hidden = jnp.concatenate([gate_hidden, rest_hidden], axis=1)
    delta_normed = jnp.dot(delta_hidden, joined_weight.T, preferred_element_type=f32)
    delta_embed = normalize_back(delta_normed, normed, inverse) + cotangent.astype(f32)
    delta_low = delta_embed.astype(low)
    cold_event = jnp.dot(delta_low, cold_projection.T, preferred_element_type=f32).astype(low)
    event = jnp.where(
        is_hot[:, None], delta_low, jnp.pad(cold_event, ((0, 0), (0, width - cold_width)))
    )
    row_buffer = lax.dot_general(
        chosen.astype(low), event, (((0,), (0,)), ((), ())), preferred_element_type=low
    ).reshape(devices, capacity, width)
    cold_low = jnp.where(is_cold[:, None], cold_vector, jnp.zeros((), low))
    projection_part = lax.dot_general(
        cold_low, delta_low, (((0,), (0,)), ((), ())), preferred_element_type=f32
    ).astype(low)
    sent = jnp.concatenate(
        [row_buffer, projection_part.reshape(devices, cold_width // devices, width)], axis=1
    )
    arrived = lax.all_to_all(sent, everyone, split_axis=0, concat_axis=0, tiled=True)
    arrived_rows = arrived[:, :capacity].reshape(devices * capacity, width)
    hot_gradient = lax.dot_general(
        hot_select.astype(low), arrived_rows, (((0,), (0,)), ((), ())), preferred_element_type=f32
    )
    cold_gradient = lax.dot_general(
        cold_select.astype(low),
        arrived_rows[:, :cold_width],
        (((0,), (0,)), ((), ())),
        preferred_element_type=f32,
    )
    projection_mine = jnp.sum(arrived[:, capacity:].astype(f32), axis=0).astype(low)
    projection_all = gather_blocks(gather_blocks(projection_mine, "dp"), "cp")
    projection_all = projection_all.transpose(1, 0, 2, 3).reshape(cold_width, width)
    norm_scale = (tokens * devices) ** (-0.5)
    output_sum = first[:, :share].reshape(width, width)
    gate_sum = first[:, share:].reshape(1, width, width)
    rest_sum = second.reshape(group, 3, share, width).transpose(1, 0, 2, 3)
    joined_sum = jnp.concatenate([gate_sum, rest_sum.reshape(3, width, width)], axis=0)
    joined_sum = joined_sum.reshape(4 * width, width).T
    return (
        layer_out,
        hot_gradient,
        cold_gradient,
        projection_all.astype(f32) * norm_scale,
        joined_sum.astype(f32) * norm_scale,
        output_sum.astype(f32) * norm_scale,
    )


def solution(mesh):
    placed = (
        P(("dp", "cp"), None),
        P(("dp", "cp")),
        P(("dp", "cp"), None),
        P(("dp", "cp"), None),
        P(),
        P(),
        P(),
        P(("dp", "cp"), None),
    )
    return jax.shard_map(
        local,
        mesh=mesh,
        in_specs=placed,
        out_specs=(
            P(("dp", "cp"), None),
            P(("dp", "cp"), None),
            P(("dp", "cp"), None),
            P(),
            P(),
            P(),
        ),
        check_vma=False,
    )
```

```python
import functools
import math

import jax
import jax.numpy as jnp
from jax import lax
from jax.experimental import pallas as pl
from jax.experimental.pallas import tpu as pltpu
from jax.sharding import PartitionSpec as P

HEADS = 8
LANES = 128


EPSILON = 1e-05
low = jnp.bfloat16
f32 = jnp.float32
SMEM = pl.BlockSpec(memory_space=pltpu.SMEM)
VMEM = pl.BlockSpec(memory_space=pltpu.VMEM)


def sigmoid(values):
    return 0.5 + 0.5 * jnp.tanh(0.5 * values)


def silu(values):
    return values * sigmoid(values)


def silu_slope(values):
    sigmoid_v = sigmoid(values)
    return sigmoid_v * (1.0 + values * (1.0 - sigmoid_v))


def layer_normalize(values):
    average = jnp.mean(values, axis=-1, keepdims=True)
    centred = values - average
    inverse = lax.rsqrt(jnp.mean(centred * centred, axis=-1, keepdims=True) + EPSILON)
    return (centred * inverse, inverse)


def normalize_back(gradient, normed, inverse):
    first_term = jnp.mean(gradient, axis=-1, keepdims=True)
    second_term = jnp.mean(gradient * normed, axis=-1, keepdims=True)
    return (gradient - first_term - normed * second_term) * inverse


def dot(left, right, contract=(1, 0)):
    dims = (((contract[0],), (contract[1],)), ((), ()))
    return lax.dot_general(left, right, dims, preferred_element_type=f32)


def power_of_two(count):
    return count & (count - 1) == 0


def source_of(here, step, count):
    if power_of_two(count):
        return here ^ step
    return (here + count - step) % count


def target_of(here, step, count):
    if power_of_two(count):
        return here ^ step
    return (here + step) % count


def exchange(block, axis, step):
    count = lax.axis_size(axis)
    pairs = [(i, target_of(i, step, count)) for i in range(count)]
    return lax.ppermute(block, axis, pairs)


def arrival_order(count):
    if not power_of_two(count) or count < 4:
        return list(range(count))
    return list(range(0, count, 2)) + list(range(1, count, 2))


def gather_pieces(block, axis):
    count = lax.axis_size(axis)
    if not power_of_two(count) or count < 4:
        return [block] + [exchange(block, axis, step) for step in range(1, count)]
    near = [block] + [exchange(block, axis, step) for step in range(2, count, 2)]
    return near + [exchange(piece, axis, 1) for piece in near]


def call(kernel, operands, outs, scratch=(), flops=0, scalars=1):
    moved = sum(x.size * x.dtype.itemsize for x in list(operands) + list(outs))
    return pl.pallas_call(
        kernel,
        out_shape=outs,
        in_specs=[SMEM] * scalars + [VMEM] * (len(operands) - scalars),
        out_specs=[VMEM] * len(outs),
        scratch_shapes=list(scratch),
        cost_estimate=pl.CostEstimate(flops=flops, bytes_accessed=moved, transcendentals=0),
        compiler_params=pltpu.CompilerParams(vmem_limit_bytes=56 << 20),
    )(*operands)


def shaped(shape, dtype):
    return jax.ShapeDtypeStruct(shape, dtype)


def tile(index, size=LANES):
    return pl.ds(pl.multiple_of(index * size, size), size)


def head_masks(rows, head_size):
    lane = lax.broadcasted_iota(jnp.int32, (rows, LANES), 1)
    return [lane // head_size == n for n in range(LANES // head_size)]


def only(mask, values):
    return jnp.where(mask, values, jnp.zeros((), values.dtype))


def merge(masks, parts):
    result = parts[-1]
    for mask, part in zip(masks[:-1], parts[:-1]):
        result = jnp.where(mask, part, result)
    return result


def fill_mask(mask_ref, here, order, group, tokens, forward):
    row = lax.broadcasted_iota(jnp.int32, (tokens, tokens), 0)
    column = lax.broadcasted_iota(jnp.int32, (tokens, tokens), 1)
    for n, step in enumerate(order):
        gap = (here - source_of(here, step, group)) * tokens
        allowed = (column - row <= gap) if forward else (column - row >= gap)
        mask_ref[:, n * tokens : (n + 1) * tokens] = allowed.astype(f32)


def hidden_kernel(here_ref, normed_ref, weight_ref, hidden_ref, active_ref):
    hidden = dot(normed_ref[...], weight_ref[...])
    hidden_ref[...] = hidden
    active_ref[...] = silu(hidden).astype(low)


def forward_kernel(group, scale, head_size, *refs):
    here_ref, pieces = refs[0], refs[1 : 1 + group]
    weight_ref, active_ref, hidden_ref, embedded_ref, mix_ref, cotangent_ref = refs[1 + group : 7 + group]
    out_ref, delta_ref, gate_ref, early_ref, all_ref, normed_scr, mask_scr, att_scr = refs[7 + group :]
    tokens, width = embedded_ref.shape
    order = arrival_order(group)
    here = here_ref[0]
    for n in range(1, group):
        normed_scr[n] = pieces[n][...]
    fill_mask(mask_scr, here, order, group, tokens, True)
    all_ref[0:tokens, :] = active_ref[:, width:]

    def project(n, carry):
        hidden = dot(normed_scr[n], weight_ref[:, width:])
        all_ref[tile(n, tokens), :] = silu(hidden).astype(low)
        return carry

    lax.fori_loop(1, group, project, 0)
    masks = head_masks(tokens, head_size)

    def attend(n, carry):
        values = all_ref[:, tile(n)]
        queries = all_ref[0:tokens, tile(n + width // LANES)]
        keys = all_ref[:, tile(n + 2 * width // LANES)]
        parts = []
        for mask in masks:
            scores = dot(only(mask, queries), keys, (1, 1)) * scale
            weights = (silu(scores) * mask_scr[...]).astype(low)
            parts.append(dot(weights, values))
        att_scr[:, tile(n)] = merge(masks, parts)
        return carry

    lax.fori_loop(0, width // LANES, attend, 0)
    mixed, inverse_mix = layer_normalize(att_scr[...])
    gate = active_ref[:, :width].astype(f32)
    gated = (mixed * gate).astype(low)
    out_ref[...] = (embedded_ref[...] + dot(gated, mix_ref[...])).astype(low)
    delta_gated = dot(cotangent_ref[...], mix_ref[...], (1, 1))
    delta_ref[...] = normalize_back(delta_gated * gate, mixed, inverse_mix).astype(low)
    gate_hidden = (delta_gated * mixed * silu_slope(hidden_ref[:, :width])).astype(low)
    gate_ref[...] = gate_hidden
    share = width // group
    gated_t = gated.astype(f32).T.astype(low)
    hidden_t = gate_hidden.astype(f32).T.astype(low)
    for n in range(group):
        early_ref[n, 0:share] = gated_t[n * share : (n + 1) * share]
        early_ref[n, share : 2 * share] = hidden_t[n * share : (n + 1) * share]


def query_kernel(group, scale, head_size, *refs):
    here_ref, all_ref, delta_ref, hidden_ref, out_ref, mask_scr = refs
    tokens, width = delta_ref.shape
    fill_mask(mask_scr, here_ref[0], arrival_order(group), group, tokens, True)
    masks = head_masks(tokens, head_size)

    def step(n, carry):
        values = all_ref[:, tile(n)]
        queries = all_ref[0:tokens, tile(n + width // LANES)]
        keys = all_ref[:, tile(n + 2 * width // LANES)]
        delta = delta_ref[:, tile(n)]
        parts = []
        for mask in masks:
            scores = dot(only(mask, queries), keys, (1, 1)) * scale
            change = dot(only(mask, delta), values, (1, 1))
            change = (change * silu_slope(scores) * (mask_scr[...] * scale)).astype(low)
            parts.append(dot(change, keys))
        slope = silu_slope(hidden_ref[:, tile(n + 2 * width // LANES)])
        out_ref[:, tile(n)] = (merge(masks, parts) * slope).astype(low)
        return carry

    lax.fori_loop(0, width // LANES, step, 0)


def key_kernel(group, scale, head_size, *refs):
    here_ref, pieces = refs[0], refs[1 : 1 + group]
    all_ref, hidden_ref, query_ref, rest_ref, late_ref, delta_scr, mask_scr = refs[1 + group :]
    tokens, width = query_ref.shape
    for n in range(group):
        delta_scr[n * tokens : (n + 1) * tokens, :] = pieces[n][...]
    fill_mask(mask_scr, here_ref[0], arrival_order(group), group, tokens, False)
    masks = head_masks(tokens, head_size)
    tiles = width // LANES

    def step(n, carry):
        values = all_ref[0:tokens, tile(n)]
        queries = all_ref[:, tile(n + tiles)]
        keys = all_ref[0:tokens, tile(n + 2 * tiles)]
        delta = delta_scr[:, tile(n)]
        value_parts, key_parts = [], []
        for mask in masks:
            scores = dot(only(mask, keys), queries, (1, 1)) * scale
            change = dot(only(mask, values), delta, (1, 1))
            sigmoid_v = sigmoid(scores)
            weights = (scores * sigmoid_v * mask_scr[...]).astype(low)
            slope = sigmoid_v * (1.0 + scores * (1.0 - sigmoid_v))
            change = (change * slope * (mask_scr[...] * scale)).astype(low)
            value_parts.append(dot(weights, delta))
            key_parts.append(dot(change, queries))
        for parts, at in ((value_parts, 0), (key_parts, 2)):
            slope = silu_slope(hidden_ref[:, tile(n + (at + 1) * tiles)])
            rest_ref[:, tile(n + at * tiles)] = (merge(masks, parts) * slope).astype(low)
        return carry

    lax.fori_loop(0, tiles, step, 0)
    rest_ref[:, width : 2 * width] = query_ref[...]
    late_ref[...] = rest_ref[...].astype(f32).T.astype(low)


def row_kernel(head_rows, capacity, *refs):
    here_ref, gate_ref, rest_ref, weight_ref, embedded_ref, cotangent_ref = refs[:6]
    vector_ref, slot_ref, place_ref, cold_ref, sent_ref = refs[6:]
    tokens, width = embedded_ref.shape
    cold_width = cold_ref.shape[0]
    devices, padded, _ = sent_ref.shape
    delta_normed = dot(gate_ref[...], weight_ref[:, :width], (1, 1))
    delta_normed += dot(rest_ref[...], weight_ref[:, width:], (1, 1))
    normed, inverse = layer_normalize(embedded_ref[...])
    delta_embed = normalize_back(delta_normed, normed, inverse) + cotangent_ref[...].astype(f32)
    delta_low = delta_embed.astype(low)
    cold = slot_ref[...] >= head_rows
    cold_event = dot(delta_low, cold_ref[...], (1, 1))
    hot_event = jnp.where(cold, 0.0, delta_embed)
    narrow = jnp.where(cold, cold_event, hot_event[:, :cold_width])
    event = jnp.concatenate([narrow, hot_event[:, cold_width:]], axis=1).astype(low)
    place = lax.broadcasted_iota(jnp.int32, (tokens, devices * padded), 1)
    chosen = (place == place_ref[...]).astype(f32).astype(low)
    sent_ref[...] = dot(chosen, event, (0, 0)).astype(low).reshape(sent_ref.shape)
    cold_rows = jnp.where(cold, vector_ref[:, :cold_width].astype(f32), 0.0).astype(low)
    part = dot(cold_rows, delta_low, (0, 0)).astype(low)
    each = cold_width // devices
    for n in range(devices):
        sent_ref[n, capacity : capacity + each] = part[n * each : (n + 1) * each]


def weight_kernel(group, count, halves, *refs):
    here_ref, moved_ref = refs[:2]
    sides = [refs[2 + n * group : 2 + (n + 1) * group] for n in range(halves)]
    own_ref = refs[2 + halves * group]
    sends = refs[3 + halves * group : 2 + halves * group + count]
    part_scr = refs[2 + halves * group + count]
    here, outer = here_ref[0], here_ref[1]
    rows = moved_ref.shape[1] // halves
    chunk = own_ref.shape[0]
    totals = [None] * halves
    for n, step in enumerate(arrival_order(group)):
        block = moved_ref[source_of(here, step, group)]
        for half in range(halves):
            term = dot(block[half * rows : (half + 1) * rows], sides[half][n][...])
            totals[half] = term if n == 0 else totals[half] + term
    total = totals[0] if halves == 1 else jnp.concatenate(totals, axis=0)
    for n in range(count):
        part_scr[n] = total[n * chunk : (n + 1) * chunk]
    own_ref[...] = part_scr[outer]
    for step in range(1, count):
        sends[step - 1][...] = part_scr[target_of(outer, step, count)].astype(low)


def final_kernel(group, count, norm_scale, *refs):
    here_ref = refs[0]
    first, second = refs[1 : 1 + group], refs[1 + group : 1 + 2 * group]
    joined_ref, output_ref, first_scr, second_scr = refs[1 + 2 * group :]
    here, outer = here_ref[0], here_ref[1]
    width = output_ref.shape[0]
    for pieces, scr in ((first, first_scr), (second, second_scr)):
        chunk = scr.shape[2]
        for n, step in enumerate(arrival_order(group)):
            source = source_of(here, step, group)
            for m in range(count):
                piece = pieces[n][m * chunk : (m + 1) * chunk].astype(f32) * norm_scale
                scr[source, source_of(outer, m, count)] = piece
    share = width // group
    for n in range(group):
        block = first_scr[n].reshape(2 * share, width)
        output_ref[n * share : (n + 1) * share, :] = block[:share]
    gate = jnp.concatenate(
        [first_scr[n].reshape(2 * share, width)[share:] for n in range(group)], axis=0
    )
    joined_ref[:, :width] = gate.T
    rest = second_scr[...].reshape(3 * width, width)
    for n in range(3):
        joined_ref[:, (n + 1) * width : (n + 2) * width] = rest[n * width : (n + 1) * width].T


def weight_sum(position, moved, sides, width):
    group, count = lax.axis_size("cp"), lax.axis_size("dp")
    rows = moved.shape[1]
    chunk = rows // count
    operands = [position, moved] + [piece for side in sides for piece in side]
    outs = [shaped((chunk, width), f32)] + [shaped((chunk, width), low)] * (count - 1)
    own, *sends = call(
        functools.partial(weight_kernel, group, count, len(sides)),
        operands,
        outs,
        [pltpu.VMEM((count, chunk, width), f32)],
        2 * rows * moved.shape[2] * group * width,
    )
    for step, block in enumerate(sends, start=1):
        own = own + exchange(block, "dp", step).astype(f32)
    mine = own.astype(low)
    row = [mine] + [exchange(mine, "dp", step) for step in range(1, count)]
    return gather_pieces(jnp.concatenate(row, axis=0), "cp")


def assemble(position, first, second, norm_scale, width):
    group, count = lax.axis_size("cp"), lax.axis_size("dp")
    share = width // group
    sizes = (2 * share // count, 3 * share // count)
    if all(size % 16 == 0 for size in sizes):
        return call(
            functools.partial(final_kernel, group, count, norm_scale),
            [position] + first + second,
            [shaped((width, 4 * width), f32), shaped((width, width), f32)],
            [pltpu.VMEM((group, count, size, width), f32) for size in sizes],
        )
    whole = []
    for pieces, size in zip((first, second), sizes):
        result = jnp.zeros((group, count, size, width), low)
        for step, piece in zip(arrival_order(group), pieces):
            piece = piece.reshape(count, size, width)
            source = source_of(position[0], step, group)
            for n in range(count):
                place = (source, source_of(position[1], n, count), 0, 0)
                result = lax.dynamic_update_slice(result, piece[n][None, None], place)
        whole.append(result.reshape(group, count * size, width).astype(f32) * norm_scale)
    output = whole[0][:, :share].reshape(width, width)
    gate = whole[0][:, share:].reshape(width, width)
    return jnp.concatenate([gate, whole[1].reshape(3 * width, width)], axis=0).T, output


def local(
    row_owner,
    slot_row,
    hot_table,
    cold_table,
    cold_projection,
    joined_weight,
    output_weight,
    cotangent,
):
    tokens = slot_row.shape[0]
    width = output_weight.shape[0]
    hot_count = hot_table.shape[0]
    cold_count, cold_width = cold_table.shape
    head_size = width // HEADS
    score_scale = 1.0 / math.sqrt(head_size)
    everyone = ("dp", "cp")
    devices = lax.axis_size(everyone)
    group = lax.axis_size("cp")
    length = group * tokens
    position = jnp.stack([lax.axis_index("cp"), lax.axis_index("dp")]).astype(jnp.int32)
    capacity = 2 * tokens // devices + 2
    padded = -(-(capacity + cold_width // devices) // 8) * 8
    slots = devices * padded
    owners = row_owner[:, 0]
    is_hot = slot_row < hot_count
    named = owners[:, None] == jnp.arange(devices, dtype=jnp.int32)[None, :]
    onehot = named.astype(low)
    lower = (jnp.arange(tokens)[:, None] > jnp.arange(tokens)[None, :]).astype(low)
    earlier = jnp.dot(lower, onehot, preferred_element_type=f32)
    rank = jnp.sum(jnp.where(named, earlier, 0.0), axis=1).astype(jnp.int32)
    place = owners * padded + rank
    chosen = place[:, None] == jnp.arange(slots, dtype=jnp.int32)[None, :]
    requests = jnp.max(jnp.where(chosen, slot_row[:, None], -1), axis=0)
    asked = lax.all_to_all(
        requests.reshape(devices, padded), everyone, split_axis=0, concat_axis=0, tiled=True
    ).reshape(-1)
    hot_select = asked[:, None] == jnp.arange(hot_count, dtype=jnp.int32)[None, :]
    cold_select = asked[:, None] == jnp.arange(hot_count, hot_count + cold_count, dtype=jnp.int32)
    hot_pick = jnp.dot(hot_select.astype(low), hot_table, preferred_element_type=low)
    cold_pick = jnp.dot(cold_select.astype(low), cold_table, preferred_element_type=low)
    picked = hot_pick + jnp.pad(cold_pick, ((0, 0), (0, width - cold_width)))
    rows_back = lax.all_to_all(
        picked.reshape(devices, padded, width), everyone, split_axis=0, concat_axis=0, tiled=True
    ).reshape(slots, width)
    held_cotangent, _ = lax.optimization_barrier((cotangent, asked))
    cotangents = gather_pieces(held_cotangent, "cp")
    vector = jnp.dot(chosen.astype(low), rows_back, preferred_element_type=low)
    cold_embed = jnp.dot(vector[:, :cold_width], cold_projection, preferred_element_type=f32)
    embedded = jnp.where(is_hot[:, None], vector.astype(f32), cold_embed)
    normed_low = layer_normalize(embedded)[0].astype(low)
    normeds = gather_pieces(normed_low, "cp")
    hidden, active = call(
        hidden_kernel,
        [position, normed_low, joined_weight],
        [shaped((tokens, 4 * width), f32), shaped((tokens, 4 * width), low)],
        flops=8 * tokens * width * width,
    )
    share = width // group
    work = 2 * tokens * length * width
    mask = pltpu.VMEM((tokens, length), f32)
    layer_out, delta_attended, gate_hidden, early, everything = call(
        functools.partial(forward_kernel, group, score_scale, head_size),
        [position, *normeds, joined_weight, active, hidden, embedded, output_weight, cotangent],
        [
            shaped((tokens, width), low),
            shaped((tokens, width), low),
            shaped((tokens, width), low),
            shaped((group, 2 * share, tokens), low),
            shaped((length, 3 * width), low),
        ],
        [pltpu.VMEM((group, tokens, width), low), mask, pltpu.VMEM((tokens, width), f32)],
        2 * work + 6 * length * width * width,
    )
    deltas = gather_pieces(delta_attended, "cp")
    query_hidden = call(
        functools.partial(query_kernel, group, score_scale, head_size),
        [position, everything, delta_attended, hidden],
        [shaped((tokens, width), low)],
        [mask],
        3 * work,
    )[0]
    early, query_hidden = lax.optimization_barrier((early, query_hidden))
    early = lax.all_to_all(early, "cp", split_axis=0, concat_axis=0, tiled=True)
    rest_hidden, late = call(
        functools.partial(key_kernel, group, score_scale, head_size),
        [position, *deltas, everything, hidden, query_hidden],
        [shaped((tokens, 3 * width), low), shaped((3 * width, tokens), low)],
        [pltpu.VMEM((length, width), low), mask],
        4 * work,
    )
    late = late.reshape(group, 3 * share, tokens)
    late = lax.all_to_all(late, "cp", split_axis=0, concat_axis=0, tiled=True)
    sent = call(
        functools.partial(row_kernel, hot_count, capacity),
        [
            position,
            gate_hidden,
            rest_hidden,
            joined_weight,
            embedded,
            cotangent,
            vector,
            slot_row[:, None],
            place[:, None],
            cold_projection,
        ],
        [shaped((devices, padded, width), low)],
        flops=8 * tokens * width * width,
    )[0]
    arrived = lax.all_to_all(sent, everyone, split_axis=0, concat_axis=0, tiled=True)
    first = weight_sum(position, early, [cotangents, normeds], width)
    second = weight_sum(position, late, [normeds], width)
    arrived_rows = arrived.reshape(slots, width)
    hot_gradient = dot(hot_select.astype(low), arrived_rows, (0, 0))
    cold_gradient = dot(cold_select.astype(low), arrived_rows[:, :cold_width], (0, 0))
    each = cold_width // devices
    mine = jnp.sum(arrived[:, capacity : capacity + each].astype(f32), axis=0).astype(low)
    copies = jnp.broadcast_to(mine[None], (devices,) + mine.shape)
    projection = lax.all_to_all(copies, everyone, split_axis=0, concat_axis=0, tiled=True)
    norm_scale = (tokens * devices) ** (-0.5)
    joined_gradient, output_gradient = assemble(position, first, second, norm_scale, width)
    return (
        layer_out,
        hot_gradient,
        cold_gradient,
        projection.reshape(cold_width, width).astype(f32) * norm_scale,
        joined_gradient,
        output_gradient,
    )


def solution(mesh):
    placed = (
        P(("dp", "cp"), None),
        P(("dp", "cp")),
        P(("dp", "cp"), None),
        P(("dp", "cp"), None),
        P(),
        P(),
        P(),
        P(("dp", "cp"), None),
    )
    return jax.shard_map(
        local,
        mesh=mesh,
        in_specs=placed,
        out_specs=(
            P(("dp", "cp"), None),
            P(("dp", "cp"), None),
            P(("dp", "cp"), None),
            P(),
            P(),
            P(),
        ),
        check_vma=False,
    )
```

```python
import functools
import math

import jax
import jax.numpy as jnp
from jax import lax
from jax.experimental import pallas as pl
from jax.experimental.pallas import tpu as pltpu
from jax.sharding import PartitionSpec as P


HEADS = 8
LANES = 128


EPSILON = 1e-05
low = jnp.bfloat16
f32 = jnp.float32
SMEM = pl.BlockSpec(memory_space=pltpu.SMEM)
VMEM = pl.BlockSpec(memory_space=pltpu.VMEM)


def sigmoid(values):
    return 0.5 + 0.5 * jnp.tanh(0.5 * values)


def silu(values):
    return values * sigmoid(values)


def silu_slope(values):
    sigmoid_v = sigmoid(values)
    return sigmoid_v * (1.0 + values * (1.0 - sigmoid_v))


def layer_normalize(values):
    average = jnp.mean(values, axis=-1, keepdims=True)
    centred = values - average
    inverse = lax.rsqrt(jnp.mean(centred * centred, axis=-1, keepdims=True) + EPSILON)
    return (centred * inverse, inverse)


def normalize_back(gradient, normed, inverse):
    first_term = jnp.mean(gradient, axis=-1, keepdims=True)
    second_term = jnp.mean(gradient * normed, axis=-1, keepdims=True)
    return (gradient - first_term - normed * second_term) * inverse


def dot(left, right, contract=(1, 0)):
    dims = (((contract[0],), (contract[1],)), ((), ()))
    return lax.dot_general(left, right, dims, preferred_element_type=f32)


def power_of_two(count):
    return count & (count - 1) == 0


def source_of(here, step, count):
    if power_of_two(count):
        return here ^ step
    return (here + count - step) % count


def target_of(here, step, count):
    if power_of_two(count):
        return here ^ step
    return (here + step) % count


def exchange(block, axis, step):
    count = lax.axis_size(axis)
    pairs = [(i, target_of(i, step, count)) for i in range(count)]
    return lax.ppermute(block, axis, pairs)


def arrival_order(count):
    if not power_of_two(count) or count < 4:
        return list(range(count))
    return list(range(0, count, 2)) + list(range(1, count, 2))


def gather_pieces(block, axis, after=None):
    count = lax.axis_size(axis)
    if not power_of_two(count) or count < 4:
        return [block] + [exchange(block, axis, step) for step in range(1, count)]
    near = [block]
    for step in range(2, count, 2):
        near.append(exchange(block, axis, step))
    if after is not None:
        near = list(lax.optimization_barrier((*near, *after))[: len(near)])
    return near + [exchange(piece, axis, 1) for piece in near]


def call(kernel, operands, outs, scratch=(), flops=0, scalars=1, limit=24):
    moved = sum(x.size * x.dtype.itemsize for x in list(operands) + list(outs))
    return pl.pallas_call(
        kernel,
        out_shape=outs,
        in_specs=[SMEM] * scalars + [VMEM] * (len(operands) - scalars),
        out_specs=[VMEM] * len(outs),
        scratch_shapes=list(scratch),
        cost_estimate=pl.CostEstimate(flops=flops, bytes_accessed=moved, transcendentals=0),
        compiler_params=pltpu.CompilerParams(vmem_limit_bytes=limit << 20),
    )(*operands)


def shaped(shape, dtype):
    return jax.ShapeDtypeStruct(shape, dtype)


def tile(index, size=LANES):
    return pl.ds(pl.multiple_of(index * size, size), size)


def head_masks(rows, head_size):
    lane = lax.broadcasted_iota(jnp.int32, (rows, LANES), 1)
    return [lane // head_size == n for n in range(LANES // head_size)]


def only(mask, values):
    return jnp.where(mask, values, jnp.zeros((), values.dtype))


def merge(masks, parts):
    result = parts[-1]
    for mask, part in zip(masks[:-1], parts[:-1]):
        result = jnp.where(mask, part, result)
    return result


def fill_mask(mask_ref, here, order, group, tokens, forward):
    row = lax.broadcasted_iota(jnp.int32, (tokens, tokens), 0)
    column = lax.broadcasted_iota(jnp.int32, (tokens, tokens), 1)
    for n, step in enumerate(order):
        gap = (here - source_of(here, step, group)) * tokens
        allowed = (column - row <= gap) if forward else (column - row >= gap)
        mask_ref[:, n * tokens : (n + 1) * tokens] = allowed.astype(f32)


def hidden_kernel(here_ref, normed_ref, weight_ref, hidden_ref, active_ref):
    hidden = dot(normed_ref[...], weight_ref[...])
    hidden_ref[...] = hidden
    active_ref[...] = silu(hidden).astype(low)


def forward_kernel(group, scale, head_size, *refs):
    here_ref, pieces = refs[0], refs[1 : 1 + group]
    weight_ref, active_ref, hidden_ref, embedded_ref, mix_ref, cotangent_ref = refs[1 + group : 7 + group]
    out_ref, delta_ref, gate_ref, early_ref, all_ref, normed_scr, mask_scr, att_scr = refs[7 + group :]
    tokens, width = embedded_ref.shape
    order = arrival_order(group)
    here = here_ref[0]
    for n in range(1, group):
        normed_scr[n] = pieces[n][...]
    fill_mask(mask_scr, here, order, group, tokens, True)
    all_ref[0:tokens, :width] = active_ref[:, width : 2 * width]
    all_ref[0:tokens, width:] = active_ref[:, 3 * width :]

    def project(n, carry):
        hidden = dot(normed_scr[n], weight_ref[:, width : 2 * width])
        all_ref[tile(n, tokens), :width] = silu(hidden).astype(low)
        hidden = dot(normed_scr[n], weight_ref[:, 3 * width :])
        all_ref[tile(n, tokens), width:] = silu(hidden).astype(low)
        return carry

    lax.fori_loop(1, group, project, 0)
    masks = head_masks(tokens, head_size)

    def attend(n, carry):
        values = all_ref[:, tile(n)]
        queries = active_ref[:, tile(n + 2 * width // LANES)]
        keys = all_ref[:, tile(n + width // LANES)]
        parts = []
        for mask in masks:
            scores = dot(only(mask, queries), keys, (1, 1)) * scale
            weights = (silu(scores) * mask_scr[...]).astype(low)
            parts.append(dot(weights, values))
        att_scr[:, tile(n)] = merge(masks, parts)
        return carry

    lax.fori_loop(0, width // LANES, attend, 0)
    mixed, inverse_mix = layer_normalize(att_scr[...])
    gate = active_ref[:, :width].astype(f32)
    gated = (mixed * gate).astype(low)
    out_ref[...] = (embedded_ref[...] + dot(gated, mix_ref[...])).astype(low)
    delta_gated = dot(cotangent_ref[...], mix_ref[...], (1, 1))
    delta_ref[...] = normalize_back(delta_gated * gate, mixed, inverse_mix).astype(low)
    gate_hidden = (delta_gated * mixed * silu_slope(hidden_ref[:, :width])).astype(low)
    gate_ref[...] = gate_hidden
    share = width // group
    gated_t = gated.astype(f32).T.astype(low)
    hidden_t = gate_hidden.astype(f32).T.astype(low)
    for n in range(group):
        early_ref[n, 0:share] = gated_t[n * share : (n + 1) * share]
        early_ref[n, share : 2 * share] = hidden_t[n * share : (n + 1) * share]


def query_kernel(group, scale, head_size, *refs):
    here_ref, pieces = refs[0], refs[1 : 1 + group]
    weight_ref, active_ref, all_ref, delta_ref, hidden_ref = refs[1 + group : 6 + group]
    out_ref, queries_ref, normed_scr, mask_scr = refs[6 + group :]
    tokens, width = delta_ref.shape
    for n in range(1, group):
        normed_scr[n] = pieces[n][...]
    queries_ref[0:tokens, :] = active_ref[:, 2 * width : 3 * width]

    def project(n, carry):
        hidden = dot(normed_scr[n], weight_ref[:, 2 * width : 3 * width])
        queries_ref[tile(n, tokens), :] = silu(hidden).astype(low)
        return carry

    lax.fori_loop(1, group, project, 0)
    fill_mask(mask_scr, here_ref[0], arrival_order(group), group, tokens, True)
    masks = head_masks(tokens, head_size)

    def step(n, carry):
        values = all_ref[:, tile(n)]
        queries = active_ref[:, tile(n + 2 * width // LANES)]
        keys = all_ref[:, tile(n + width // LANES)]
        delta = delta_ref[:, tile(n)]
        parts = []
        for mask in masks:
            scores = dot(only(mask, queries), keys, (1, 1)) * scale
            change = dot(only(mask, delta), values, (1, 1))
            change = (change * silu_slope(scores) * (mask_scr[...] * scale)).astype(low)
            parts.append(dot(change, keys))
        slope = silu_slope(hidden_ref[:, tile(n + 2 * width // LANES)])
        out_ref[:, tile(n)] = (merge(masks, parts) * slope).astype(low)
        return carry

    lax.fori_loop(0, width // LANES, step, 0)


def key_kernel(group, scale, head_size, *refs):
    here_ref, pieces = refs[0], refs[1 : 1 + group]
    active_ref, queries_ref, hidden_ref, query_ref, early_ref = refs[1 + group : 6 + group]
    rest_ref, columns_ref, delta_scr, mask_scr = refs[6 + group :]
    tokens, width = query_ref.shape
    for n in range(group):
        delta_scr[n * tokens : (n + 1) * tokens, :] = pieces[n][...]
    fill_mask(mask_scr, here_ref[0], arrival_order(group), group, tokens, False)
    masks = head_masks(tokens, head_size)
    tiles = width // LANES

    def step(n, carry):
        values = active_ref[:, tile(n + tiles)]
        queries = queries_ref[:, tile(n)]
        keys = active_ref[:, tile(n + 3 * tiles)]
        delta = delta_scr[:, tile(n)]
        value_parts, key_parts = [], []
        for mask in masks:
            scores = dot(only(mask, keys), queries, (1, 1)) * scale
            change = dot(only(mask, values), delta, (1, 1))
            sigmoid_v = sigmoid(scores)
            weights = (scores * sigmoid_v * mask_scr[...]).astype(low)
            slope = sigmoid_v * (1.0 + scores * (1.0 - sigmoid_v))
            change = (change * slope * (mask_scr[...] * scale)).astype(low)
            value_parts.append(dot(weights, delta))
            key_parts.append(dot(change, queries))
        for parts, at in ((value_parts, 0), (key_parts, 2)):
            slope = silu_slope(hidden_ref[:, tile(n + (at + 1) * tiles)])
            rest_ref[:, tile(n + at * tiles)] = (merge(masks, parts) * slope).astype(low)
        return carry

    lax.fori_loop(0, tiles, step, 0)
    rest_ref[:, width : 2 * width] = query_ref[...]
    late = rest_ref[...].astype(f32).T.astype(low)
    share = width // group
    for n in range(group):
        columns_ref[n, : 2 * share] = early_ref[n]
        columns_ref[n, 2 * share :] = late[3 * n * share : 3 * (n + 1) * share]


def row_kernel(head_rows, capacity, *refs):
    _, gate_ref, rest_ref, weight_ref, embedded_ref, cotangent_ref = refs[:6]
    vector_ref, slot_ref, place_ref, cold_ref, sent_ref = refs[6:]
    tokens, width = embedded_ref.shape
    cold_width = cold_ref.shape[0]
    devices, padded, _ = sent_ref.shape
    delta_normed = dot(gate_ref[...], weight_ref[:, :width], (1, 1))
    delta_normed += dot(rest_ref[...], weight_ref[:, width:], (1, 1))
    normed, inverse = layer_normalize(embedded_ref[...])
    delta_embed = normalize_back(delta_normed, normed, inverse) + cotangent_ref[...].astype(f32)
    delta_low = delta_embed.astype(low)
    cold = slot_ref[...] >= head_rows
    cold_event = dot(delta_low, cold_ref[...], (1, 1))
    hot_event = jnp.where(cold, 0.0, delta_embed)
    narrow = jnp.where(cold, cold_event, hot_event[:, :cold_width])
    event = jnp.concatenate([narrow, hot_event[:, cold_width:]], axis=1).astype(low)
    place = lax.broadcasted_iota(jnp.int32, (tokens, devices * padded), 1)
    chosen = (place == place_ref[...]).astype(f32).astype(low)
    sent_ref[...] = dot(chosen, event, (0, 0)).astype(low).reshape(sent_ref.shape)
    cold_rows = jnp.where(cold, vector_ref[:, :cold_width].astype(f32), 0.0).astype(low)
    part = dot(cold_rows, delta_low, (0, 0)).astype(low)
    each = cold_width // devices
    for n in range(devices):
        sent_ref[n, capacity : capacity + each] = part[n * each : (n + 1) * each]


def weight_kernel(group, count, *refs):
    here_ref, moved_ref = refs[:2]
    cotangents, normeds = refs[2 : 2 + group], refs[2 + group : 2 + 2 * group]
    own_ref = refs[2 + 2 * group]
    sends = refs[3 + 2 * group : 2 + 2 * group + count]
    part_scr = refs[2 + 2 * group + count]
    here, outer = here_ref[0], here_ref[1]
    share = moved_ref.shape[1] // 5
    chunk = own_ref.shape[0]
    top = bottom = None
    for n, step in enumerate(arrival_order(group)):
        source = source_of(here, step, group)
        first = dot(moved_ref[source, :share], cotangents[n][...])
        second = dot(moved_ref[source, share:], normeds[n][...])
        top = first if n == 0 else top + first
        bottom = second if n == 0 else bottom + second
    total = jnp.concatenate([top, bottom], axis=0)
    for n in range(count):
        part_scr[n] = total[n * chunk : (n + 1) * chunk]
    own_ref[...] = part_scr[outer]
    for step in range(1, count):
        sends[step - 1][...] = part_scr[target_of(outer, step, count)].astype(low)


def final_kernel(group, count, norm_scale, *refs):
    here_ref, pieces = refs[0], refs[1 : 1 + group]
    joined_ref, output_ref, piece_scr = refs[1 + group :]
    here, outer = here_ref[0], here_ref[1]
    width = output_ref.shape[0]
    chunk = piece_scr.shape[2]
    for n, step in enumerate(arrival_order(group)):
        source = source_of(here, step, group)
        for m in range(count):
            part = pieces[n][m * chunk : (m + 1) * chunk]
            piece_scr[source, source_of(outer, m, count)] = part
    share = width // group
    row = lax.broadcasted_iota(jnp.int32, (width, width), 0)
    column = lax.broadcasted_iota(jnp.int32, (width, width), 1)
    unit = (row == column).astype(f32).astype(low)
    blocks = [piece_scr[n].reshape(5 * share, width) for n in range(group)]
    for n in range(group):
        output_ref[n * share : (n + 1) * share, :] = blocks[n][:share].astype(f32) * norm_scale
    gate = jnp.concatenate([block[share : 2 * share] for block in blocks], axis=0)
    joined_ref[:, :width] = dot(unit, gate, (1, 1)) * norm_scale
    rest = jnp.concatenate([block[2 * share :] for block in blocks], axis=0)
    for n in range(3):
        columns = dot(unit, rest[n * width : (n + 1) * width], (1, 1)) * norm_scale
        joined_ref[:, (n + 1) * width : (n + 2) * width] = columns


def scatter_kernel(capacity, each, *refs):
    _, asked_ref, arrived_ref, hot_ref, cold_ref, mine_ref = refs
    devices, padded, width = arrived_ref.shape
    slots = devices * padded
    hot_count, cold_width = hot_ref.shape[0], cold_ref.shape[1]
    rows = arrived_ref[...].reshape(slots, width)
    asked = asked_ref[...]
    index = lax.broadcasted_iota(jnp.int32, (hot_count, slots), 0)
    for n in range(cold_ref.shape[0] // hot_count):
        chosen = (index + (n + 1) * hot_count == asked).astype(f32).astype(low)
        cold_ref[n * hot_count : (n + 1) * hot_count, :] = dot(chosen, rows[:, :cold_width])
    hot_ref[...] = dot((index == asked).astype(f32).astype(low), rows)
    total = arrived_ref[0].astype(f32)
    for n in range(1, devices):
        total = total + arrived_ref[n].astype(f32)
    mine_ref[...] = total[capacity : capacity + each].astype(low)


def assemble(position, pieces, norm_scale, width):
    group, count = lax.axis_size("cp"), lax.axis_size("dp")
    share = width // group
    size = 5 * share // count
    if size % 16 == 0:
        return call(
            functools.partial(final_kernel, group, count, norm_scale),
            [position] + pieces,
            [shaped((width, 4 * width), f32), shaped((width, width), f32)],
            [pltpu.VMEM((group, count, size, width), low)],
        )
    result = jnp.zeros((group, count, size, width), low)
    for step, piece in zip(arrival_order(group), pieces):
        piece = piece.reshape(count, size, width)
        source = source_of(position[0], step, group)
        for n in range(count):
            place = (source, source_of(position[1], n, count), 0, 0)
            result = lax.dynamic_update_slice(result, piece[n][None, None], place)
    whole = result.reshape(group, count * size, width).astype(f32) * norm_scale
    output = whole[:, :share].reshape(width, width)
    gate = whole[:, share : 2 * share].reshape(width, width)
    rest = whole[:, 2 * share :].reshape(3 * width, width)
    return jnp.concatenate([gate, rest], axis=0).T, output


def local(
    row_owner,
    slot_row,
    hot_table,
    cold_table,
    cold_projection,
    joined_weight,
    output_weight,
    cotangent,
):
    tokens = slot_row.shape[0]
    width = output_weight.shape[0]
    hot_count = hot_table.shape[0]
    cold_count, cold_width = cold_table.shape
    head_size = width // HEADS
    score_scale = 1.0 / math.sqrt(head_size)
    everyone = ("dp", "cp")
    devices = lax.axis_size(everyone)
    group = lax.axis_size("cp")
    length = group * tokens
    position = jnp.stack([lax.axis_index("cp"), lax.axis_index("dp")]).astype(jnp.int32)
    capacity = 2 * tokens // devices + 2
    padded = -(-(capacity + cold_width // devices) // 8) * 8
    slots = devices * padded
    owners = row_owner[:, 0]
    is_hot = slot_row < hot_count
    named = owners[:, None] == jnp.arange(devices, dtype=jnp.int32)[None, :]
    onehot = named.astype(low)
    lower = (jnp.arange(tokens)[:, None] > jnp.arange(tokens)[None, :]).astype(low)
    earlier = jnp.dot(lower, onehot, preferred_element_type=f32)
    rank = jnp.sum(jnp.where(named, earlier, 0.0), axis=1).astype(jnp.int32)
    place = owners * padded + rank
    chosen = place[:, None] == jnp.arange(slots, dtype=jnp.int32)[None, :]
    requests = jnp.max(jnp.where(chosen, slot_row[:, None], -1), axis=0)
    asked = lax.all_to_all(
        requests.reshape(devices, padded), everyone, split_axis=0, concat_axis=0, tiled=True
    ).reshape(-1)
    hot_select = asked[:, None] == jnp.arange(hot_count, dtype=jnp.int32)[None, :]
    cold_select = asked[:, None] == jnp.arange(hot_count, hot_count + cold_count, dtype=jnp.int32)
    hot_pick = jnp.dot(hot_select.astype(low), hot_table, preferred_element_type=low)
    cold_pick = jnp.dot(cold_select.astype(low), cold_table, preferred_element_type=low)
    picked = hot_pick + jnp.pad(cold_pick, ((0, 0), (0, width - cold_width)))
    rows_back = lax.all_to_all(
        picked.reshape(devices, padded, width), everyone, split_axis=0, concat_axis=0, tiled=True
    ).reshape(slots, width)
    held_cotangent, _ = lax.optimization_barrier((cotangent, asked))
    cotangents = gather_pieces(held_cotangent, "cp")
    vector = jnp.dot(chosen.astype(low), rows_back, preferred_element_type=low)
    cold_embed = jnp.dot(vector[:, :cold_width], cold_projection, preferred_element_type=f32)
    embedded = jnp.where(is_hot[:, None], vector.astype(f32), cold_embed)
    normed_low = layer_normalize(embedded)[0].astype(low)
    hidden, active = call(
        hidden_kernel,
        [position, normed_low, joined_weight],
        [shaped((tokens, 4 * width), f32), shaped((tokens, 4 * width), low)],
        flops=8 * tokens * width * width,
    )
    normeds = gather_pieces(normed_low, "cp")
    share = width // group
    work = 2 * tokens * length * width
    mask = pltpu.VMEM((tokens, length), f32)
    layer_out, delta_attended, gate_hidden, early, everything = call(
        functools.partial(forward_kernel, group, score_scale, head_size),
        [position, *normeds, joined_weight, active, hidden, embedded, output_weight, cotangent],
        [
            shaped((tokens, width), low),
            shaped((tokens, width), low),
            shaped((tokens, width), low),
            shaped((group, 2 * share, tokens), low),
            shaped((length, 2 * width), low),
        ],
        [pltpu.VMEM((group, tokens, width), low), mask, pltpu.VMEM((tokens, width), f32)],
        2 * work + 4 * length * width * width,
    )
    query_hidden, all_queries = call(
        functools.partial(query_kernel, group, score_scale, head_size),
        [position, *normeds, joined_weight, active, everything, delta_attended, hidden],
        [shaped((tokens, width), low), shaped((length, width), low)],
        [pltpu.VMEM((group, tokens, width), low), mask],
        3 * work,
    )
    deltas = gather_pieces(delta_attended, "cp")
    rest_hidden, columns = call(
        functools.partial(key_kernel, group, score_scale, head_size),
        [position, *deltas, active, all_queries, hidden, query_hidden, early],
        [shaped((tokens, 3 * width), low), shaped((group, 5 * share, tokens), low)],
        [pltpu.VMEM((length, width), low), mask],
        4 * work,
    )
    moved = lax.all_to_all(columns, "cp", split_axis=0, concat_axis=0, tiled=True)
    sent = call(
        functools.partial(row_kernel, hot_count, capacity),
        [
            position,
            gate_hidden,
            rest_hidden,
            joined_weight,
            embedded,
            cotangent,
            vector,
            slot_row[:, None],
            place[:, None],
            cold_projection,
        ],
        [shaped((devices, padded, width), low)],
        flops=8 * tokens * width * width,
    )[0]
    arrived = lax.all_to_all(sent, everyone, split_axis=0, concat_axis=0, tiled=True)
    count = lax.axis_size("dp")
    chunk = 5 * share // count
    own, *sends = call(
        functools.partial(weight_kernel, group, count),
        [position, moved, *cotangents, *normeds],
        [shaped((chunk, width), f32)] + [shaped((chunk, width), low)] * (count - 1),
        [pltpu.VMEM((count, chunk, width), f32)],
        10 * share * length * width,
    )
    for step, block in enumerate(sends, start=1):
        own = own + exchange(block, "dp", step).astype(f32)
    mine = own.astype(low)
    line = [mine] + [exchange(mine, "dp", step) for step in range(1, count)]
    line = jnp.concatenate(line, axis=0)
    each = cold_width // devices
    hot_gradient, cold_gradient, total = call(
        functools.partial(scatter_kernel, capacity, each),
        [position, asked[None, :], arrived],
        [
            shaped((hot_count, width), f32),
            shaped((cold_count, cold_width), f32),
            shaped((each, width), low),
        ],
        flops=4 * slots * hot_count * width,
    )
    copies = jnp.broadcast_to(total[None], (devices, each, width))
    projection = lax.all_to_all(copies, everyone, split_axis=0, concat_axis=0, tiled=True)
    pieces = gather_pieces(line, "cp", (projection, hot_gradient, cold_gradient))
    norm_scale = (tokens * devices) ** (-0.5)
    joined_gradient, output_gradient = assemble(position, pieces, norm_scale, width)
    return (
        layer_out,
        hot_gradient,
        cold_gradient,
        projection.reshape(cold_width, width).astype(f32) * norm_scale,
        joined_gradient,
        output_gradient,
    )


def solution(mesh):
    placed = (
        P(("dp", "cp"), None),
        P(("dp", "cp")),
        P(("dp", "cp"), None),
        P(("dp", "cp"), None),
        P(),
        P(),
        P(),
        P(("dp", "cp"), None),
    )
    return jax.shard_map(
        local,
        mesh=mesh,
        in_specs=placed,
        out_specs=(
            P(("dp", "cp"), None),
            P(("dp", "cp"), None),
            P(("dp", "cp"), None),
            P(),
            P(),
            P(),
        ),
        check_vma=False,
    )
```

```python
import functools
import math

import jax
import jax.numpy as jnp
from jax import lax
from jax.experimental import pallas as pl
from jax.experimental.pallas import tpu as pltpu
from jax.sharding import PartitionSpec as P


HEADS = 8
LANES = 128


EPSILON = 1e-05
low = jnp.bfloat16
f32 = jnp.float32
SMEM = pl.BlockSpec(memory_space=pltpu.SMEM)
VMEM = pl.BlockSpec(memory_space=pltpu.VMEM)


def sigmoid(values):
    return 0.5 + 0.5 * jnp.tanh(0.5 * values)


def silu(values):
    return values * sigmoid(values)


def silu_slope(values):
    sigmoid_v = sigmoid(values)
    return sigmoid_v * (1.0 + values * (1.0 - sigmoid_v))


def layer_normalize(values):
    average = jnp.mean(values, axis=-1, keepdims=True)
    centred = values - average
    inverse = lax.rsqrt(jnp.mean(centred * centred, axis=-1, keepdims=True) + EPSILON)
    return (centred * inverse, inverse)


def normalize_back(gradient, normed, inverse):
    first_term = jnp.mean(gradient, axis=-1, keepdims=True)
    second_term = jnp.mean(gradient * normed, axis=-1, keepdims=True)
    return (gradient - first_term - normed * second_term) * inverse


def dot(left, right, contract=(1, 0)):
    dims = (((contract[0],), (contract[1],)), ((), ()))
    return lax.dot_general(left, right, dims, preferred_element_type=f32)


def power_of_two(count):
    return count & (count - 1) == 0


def source_of(here, step, count):
    if power_of_two(count):
        return here ^ step
    return (here + count - step) % count


def target_of(here, step, count):
    if power_of_two(count):
        return here ^ step
    return (here + step) % count


def exchange(block, axis, step):
    count = lax.axis_size(axis)
    pairs = [(i, target_of(i, step, count)) for i in range(count)]
    return lax.ppermute(block, axis, pairs)


def arrival_order(count):
    if not power_of_two(count) or count < 4:
        return list(range(count))
    return list(range(0, count, 2)) + list(range(1, count, 2))


def gather_pieces(block, axis, after=None):
    count = lax.axis_size(axis)
    if not power_of_two(count) or count < 4:
        return [block] + [exchange(block, axis, step) for step in range(1, count)]
    near = [block]
    for step in range(2, count, 2):
        near.append(exchange(block, axis, step))
    if after is not None:
        near = list(lax.optimization_barrier((*near, *after))[: len(near)])
    return near + [exchange(piece, axis, 1) for piece in near]


def call(kernel, operands, outs, scratch=(), flops=0, scalars=1, limit=24):
    moved = sum(x.size * x.dtype.itemsize for x in list(operands) + list(outs))
    return pl.pallas_call(
        kernel,
        out_shape=outs,
        in_specs=[SMEM] * scalars + [VMEM] * (len(operands) - scalars),
        out_specs=[VMEM] * len(outs),
        scratch_shapes=list(scratch),
        cost_estimate=pl.CostEstimate(flops=flops, bytes_accessed=moved, transcendentals=0),
        compiler_params=pltpu.CompilerParams(vmem_limit_bytes=limit << 20),
    )(*operands)


def shaped(shape, dtype):
    return jax.ShapeDtypeStruct(shape, dtype)


def tile(index, size=LANES):
    return pl.ds(pl.multiple_of(index * size, size), size)


def head_masks(rows, head_size):
    lane = lax.broadcasted_iota(jnp.int32, (rows, LANES), 1)
    return [lane // head_size == n for n in range(LANES // head_size)]


def only(mask, values):
    return jnp.where(mask, values, jnp.zeros((), values.dtype))


def merge(masks, parts):
    result = parts[-1]
    for mask, part in zip(masks[:-1], parts[:-1]):
        result = jnp.where(mask, part, result)
    return result


def fill_mask(mask_ref, here, order, group, tokens, forward):
    row = lax.broadcasted_iota(jnp.int32, (tokens, tokens), 0)
    column = lax.broadcasted_iota(jnp.int32, (tokens, tokens), 1)
    for n, step in enumerate(order):
        gap = (here - source_of(here, step, group)) * tokens
        allowed = (column - row <= gap) if forward else (column - row >= gap)
        mask_ref[:, n * tokens : (n + 1) * tokens] = allowed.astype(f32)


def unit_mask(size):
    row = lax.broadcasted_iota(jnp.int32, (size, size), 0)
    return row == lax.broadcasted_iota(jnp.int32, (size, size), 1)


def as_row(column):
    return jnp.sum(jnp.where(unit_mask(column.shape[0]), column, 0), axis=0, keepdims=True)


def as_column(row):
    return jnp.sum(jnp.where(unit_mask(row.shape[1]), row, 0), axis=1, keepdims=True)


def selected(flags):
    return flags.astype(f32).astype(low)


def request_kernel(here_ref, owner_ref, slot_ref, request_ref, rank_ref, column_ref):
    tokens = owner_ref.shape[0]
    devices = request_ref.shape[0]
    named = owner_ref[...] == lax.broadcasted_iota(jnp.int32, (tokens, devices), 1)
    row = lax.broadcasted_iota(jnp.int32, (tokens, tokens), 0)
    lower = selected(row > lax.broadcasted_iota(jnp.int32, (tokens, tokens), 1))
    earlier = dot(lower, selected(named))
    rank = jnp.sum(jnp.where(named, earlier, 0.0), axis=1, keepdims=True).astype(jnp.int32)
    rank_ref[...] = rank
    slot = as_column(slot_ref[...])
    column_ref[...] = slot
    ranked = rank == lax.broadcasted_iota(jnp.int32, (tokens, LANES), 1)
    code = slot + 1
    high = jnp.where(ranked, code >> 6, 0).astype(f32).astype(low)
    rest = jnp.where(ranked, code & 63, 0).astype(f32).astype(low)
    names = selected(named)
    total = dot(names, high, (0, 0)) * 64.0 + dot(names, rest, (0, 0)) - 1.0
    request_ref[...] = total.astype(jnp.int32).reshape(devices, 1, LANES)


def asked_select(asked, capacity, first, count):
    index = lax.broadcasted_iota(jnp.int32, (asked.shape[0], count), 1) + first
    parts = [selected(asked[:, n : n + 1] == index) for n in range(capacity)]
    return jnp.concatenate(parts, axis=0)


def pick_kernel(capacity, here_ref, asked_ref, hot_ref, cold_ref, out_ref):
    devices = asked_ref.shape[0]
    hot_count, width = hot_ref.shape
    cold_count, cold_width = cold_ref.shape
    asked = asked_ref[...].reshape(devices, LANES)
    hot = dot(asked_select(asked, capacity, 0, hot_count), hot_ref[...])
    cold = dot(asked_select(asked, capacity, hot_count, cold_count), cold_ref[...])
    tiles = [hot[:, n * LANES : (n + 1) * LANES] for n in range(width // LANES)]
    for n in range(cold_width // LANES):
        tiles[n] = tiles[n] + cold[:, n * LANES : (n + 1) * LANES]
    stack = jnp.concatenate(tiles, axis=0).reshape(len(tiles) * capacity, devices, LANES)
    out_ref[...] = jnp.swapaxes(stack, 0, 1).reshape(out_ref.shape).astype(low)


def embed_kernel(capacity, hot_count, *refs):
    _, owner_ref, rank_ref, slot_ref, rows_ref, cold_ref = refs[:6]
    vector_ref, embedded_ref, normed_ref = refs[6:]
    tokens, width = embedded_ref.shape
    cold_width = cold_ref.shape[0]
    tiles = width // LANES
    base = owner_ref[...] * (tiles * capacity) + rank_ref[...]
    index = lax.broadcasted_iota(jnp.int32, (tokens, rows_ref.shape[0]), 1)
    parts = [
        dot(selected(index == base + n * capacity), rows_ref[...]) for n in range(tiles)
    ]
    vector = jnp.concatenate(parts, axis=1)
    narrow = vector[:, :cold_width].astype(low)
    vector_ref[...] = narrow
    embedded = jnp.where(slot_ref[...] >= hot_count, dot(narrow, cold_ref[...]), vector)
    embedded_ref[...] = embedded
    normed_ref[...] = layer_normalize(embedded)[0].astype(low)


def hidden_kernel(here_ref, normed_ref, weight_ref, hidden_ref, active_ref):
    hidden = dot(normed_ref[...], weight_ref[...])
    hidden_ref[...] = hidden
    active_ref[...] = silu(hidden).astype(low)


def forward_kernel(group, scale, head_size, *refs):
    here_ref, pieces = refs[0], refs[1 : 1 + group]
    weight_ref, active_ref, hidden_ref, embedded_ref, mix_ref, cotangent_ref = refs[1 + group : 7 + group]
    out_ref, delta_ref, gate_ref, early_ref, all_ref, normed_scr, mask_scr, att_scr = refs[7 + group :]
    tokens, width = embedded_ref.shape
    order = arrival_order(group)
    here = here_ref[0]
    for n in range(1, group):
        normed_scr[n] = pieces[n][...]
    fill_mask(mask_scr, here, order, group, tokens, True)
    all_ref[0:tokens, :width] = active_ref[:, width : 2 * width]
    all_ref[0:tokens, width:] = active_ref[:, 3 * width :]

    def project(n, carry):
        hidden = dot(normed_scr[n], weight_ref[:, width : 2 * width])
        all_ref[tile(n, tokens), :width] = silu(hidden).astype(low)
        hidden = dot(normed_scr[n], weight_ref[:, 3 * width :])
        all_ref[tile(n, tokens), width:] = silu(hidden).astype(low)
        return carry

    lax.fori_loop(1, group, project, 0)
    masks = head_masks(tokens, head_size)

    def attend(n, carry):
        values = all_ref[:, tile(n)]
        queries = active_ref[:, tile(n + 2 * width // LANES)]
        keys = all_ref[:, tile(n + width // LANES)]
        parts = []
        for mask in masks:
            scores = dot(only(mask, queries), keys, (1, 1)) * scale
            weights = (silu(scores) * mask_scr[...]).astype(low)
            parts.append(dot(weights, values))
        att_scr[:, tile(n)] = merge(masks, parts)
        return carry

    lax.fori_loop(0, width // LANES, attend, 0)
    mixed, inverse_mix = layer_normalize(att_scr[...])
    gate = active_ref[:, :width].astype(f32)
    gated = (mixed * gate).astype(low)
    out_ref[...] = (embedded_ref[...] + dot(gated, mix_ref[...])).astype(low)
    delta_gated = dot(cotangent_ref[...], mix_ref[...], (1, 1))
    delta_ref[...] = normalize_back(delta_gated * gate, mixed, inverse_mix).astype(low)
    gate_hidden = (delta_gated * mixed * silu_slope(hidden_ref[:, :width])).astype(low)
    gate_ref[...] = gate_hidden
    share = width // group
    gated_t = gated.astype(f32).T.astype(low)
    hidden_t = gate_hidden.astype(f32).T.astype(low)
    for n in range(group):
        early_ref[n, 0:share] = gated_t[n * share : (n + 1) * share]
        early_ref[n, share : 2 * share] = hidden_t[n * share : (n + 1) * share]


def query_kernel(group, scale, head_size, *refs):
    here_ref, pieces = refs[0], refs[1 : 1 + group]
    weight_ref, active_ref, all_ref, delta_ref, hidden_ref = refs[1 + group : 6 + group]
    out_ref, queries_ref, normed_scr, mask_scr = refs[6 + group :]
    tokens, width = delta_ref.shape
    for n in range(1, group):
        normed_scr[n] = pieces[n][...]
    queries_ref[0:tokens, :] = active_ref[:, 2 * width : 3 * width]

    def project(n, carry):
        hidden = dot(normed_scr[n], weight_ref[:, 2 * width : 3 * width])
        queries_ref[tile(n, tokens), :] = silu(hidden).astype(low)
        return carry

    lax.fori_loop(1, group, project, 0)
    fill_mask(mask_scr, here_ref[0], arrival_order(group), group, tokens, True)
    masks = head_masks(tokens, head_size)

    def step(n, carry):
        values = all_ref[:, tile(n)]
        queries = active_ref[:, tile(n + 2 * width // LANES)]
        keys = all_ref[:, tile(n + width // LANES)]
        delta = delta_ref[:, tile(n)]
        parts = []
        for mask in masks:
            scores = dot(only(mask, queries), keys, (1, 1)) * scale
            change = dot(only(mask, delta), values, (1, 1))
            change = (change * silu_slope(scores) * (mask_scr[...] * scale)).astype(low)
            parts.append(dot(change, keys))
        slope = silu_slope(hidden_ref[:, tile(n + 2 * width // LANES)])
        out_ref[:, tile(n)] = (merge(masks, parts) * slope).astype(low)
        return carry

    lax.fori_loop(0, width // LANES, step, 0)


def key_kernel(group, scale, head_size, *refs):
    here_ref, pieces = refs[0], refs[1 : 1 + group]
    active_ref, queries_ref, hidden_ref, query_ref, early_ref = refs[1 + group : 6 + group]
    rest_ref, columns_ref, delta_scr, mask_scr = refs[6 + group :]
    tokens, width = query_ref.shape
    for n in range(group):
        delta_scr[n * tokens : (n + 1) * tokens, :] = pieces[n][...]
    fill_mask(mask_scr, here_ref[0], arrival_order(group), group, tokens, False)
    masks = head_masks(tokens, head_size)
    tiles = width // LANES

    def step(n, carry):
        values = active_ref[:, tile(n + tiles)]
        queries = queries_ref[:, tile(n)]
        keys = active_ref[:, tile(n + 3 * tiles)]
        delta = delta_scr[:, tile(n)]
        value_parts, key_parts = [], []
        for mask in masks:
            scores = dot(only(mask, keys), queries, (1, 1)) * scale
            change = dot(only(mask, values), delta, (1, 1))
            sigmoid_v = sigmoid(scores)
            weights = (scores * sigmoid_v * mask_scr[...]).astype(low)
            slope = sigmoid_v * (1.0 + scores * (1.0 - sigmoid_v))
            change = (change * slope * (mask_scr[...] * scale)).astype(low)
            value_parts.append(dot(weights, delta))
            key_parts.append(dot(change, queries))
        for parts, at in ((value_parts, 0), (key_parts, 2)):
            slope = silu_slope(hidden_ref[:, tile(n + (at + 1) * tiles)])
            rest_ref[:, tile(n + at * tiles)] = (merge(masks, parts) * slope).astype(low)
        return carry

    lax.fori_loop(0, tiles, step, 0)
    rest_ref[:, width : 2 * width] = query_ref[...]
    late = rest_ref[...].astype(f32).T.astype(low)
    share = width // group
    for n in range(group):
        columns_ref[n, : 2 * share] = early_ref[n]
        columns_ref[n, 2 * share :] = late[3 * n * share : 3 * (n + 1) * share]


def row_kernel(head_rows, capacity, stride, *refs):
    _, gate_ref, rest_ref, weight_ref, embedded_ref, cotangent_ref = refs[:6]
    vector_ref, owner_ref, rank_ref, slot_ref, cold_ref, sent_ref = refs[6:]
    _, width = embedded_ref.shape
    cold_width = cold_ref.shape[0]
    tiles = width // LANES
    devices = sent_ref.shape[0] // (tiles * stride)
    delta_normed = dot(gate_ref[...], weight_ref[:, :width], (1, 1))
    delta_normed += dot(rest_ref[...], weight_ref[:, width:], (1, 1))
    normed, inverse = layer_normalize(embedded_ref[...])
    delta_embed = normalize_back(delta_normed, normed, inverse) + cotangent_ref[...].astype(f32)
    delta_low = delta_embed.astype(low)
    cold = slot_ref[...] >= head_rows
    cold_event = dot(delta_low, cold_ref[...], (1, 1))
    hot_event = jnp.where(cold, 0.0, delta_embed)
    narrow = jnp.where(cold, cold_event, hot_event[:, :cold_width])
    event = jnp.concatenate([narrow, hot_event[:, cold_width:]], axis=1).astype(low)
    cold_rows = jnp.where(cold, vector_ref[...].astype(f32), 0.0).astype(low)
    part = dot(cold_rows, delta_low, (0, 0)).astype(low)
    each = cold_width // devices
    row = lax.broadcasted_iota(jnp.int32, (1, cold_width), 1)
    own = (row // each) * (tiles * stride) + capacity + row % each
    place = as_row(owner_ref[...] * (tiles * stride) + rank_ref[...])
    place = jnp.concatenate([place, own], axis=1)
    both = jnp.concatenate([event, part], axis=0)
    index = lax.broadcasted_iota(jnp.int32, (sent_ref.shape[0], place.shape[1]), 0)
    total = None
    for n in range(tiles):
        chosen = selected(index == place + n * stride)
        term = dot(chosen, both[:, n * LANES : (n + 1) * LANES])
        total = term if n == 0 else total + term
    sent_ref[...] = total.astype(low)


def weight_kernel(group, count, *refs):
    here_ref, moved_ref = refs[:2]
    cotangents, normeds = refs[2 : 2 + group], refs[2 + group : 2 + 2 * group]
    own_ref = refs[2 + 2 * group]
    sends = refs[3 + 2 * group : 2 + 2 * group + count]
    part_scr = refs[2 + 2 * group + count]
    here, outer = here_ref[0], here_ref[1]
    share = moved_ref.shape[1] // 5
    chunk = own_ref.shape[0]
    top = bottom = None
    for n, step in enumerate(arrival_order(group)):
        source = source_of(here, step, group)
        first = dot(moved_ref[source, :share], cotangents[n][...])
        second = dot(moved_ref[source, share:], normeds[n][...])
        top = first if n == 0 else top + first
        bottom = second if n == 0 else bottom + second
    total = jnp.concatenate([top, bottom], axis=0)
    for n in range(count):
        part_scr[n] = total[n * chunk : (n + 1) * chunk]
    own_ref[...] = part_scr[outer]
    for step in range(1, count):
        sends[step - 1][...] = part_scr[target_of(outer, step, count)].astype(low)


def final_kernel(group, count, norm_scale, *refs):
    here_ref, pieces = refs[0], refs[1 : 1 + group]
    joined_ref, output_ref, piece_scr = refs[1 + group :]
    here, outer = here_ref[0], here_ref[1]
    width = output_ref.shape[0]
    chunk = piece_scr.shape[2]
    for n, step in enumerate(arrival_order(group)):
        source = source_of(here, step, group)
        for m in range(count):
            part = pieces[n][m * chunk : (m + 1) * chunk]
            piece_scr[source, source_of(outer, m, count)] = part
    share = width // group
    row = lax.broadcasted_iota(jnp.int32, (width, width), 0)
    column = lax.broadcasted_iota(jnp.int32, (width, width), 1)
    unit = (row == column).astype(f32).astype(low)
    blocks = [piece_scr[n].reshape(5 * share, width) for n in range(group)]
    for n in range(group):
        output_ref[n * share : (n + 1) * share, :] = blocks[n][:share].astype(f32) * norm_scale
    gate = jnp.concatenate([block[share : 2 * share] for block in blocks], axis=0)
    joined_ref[:, :width] = dot(unit, gate, (1, 1)) * norm_scale
    rest = jnp.concatenate([block[2 * share :] for block in blocks], axis=0)
    for n in range(3):
        columns = dot(unit, rest[n * width : (n + 1) * width], (1, 1)) * norm_scale
        joined_ref[:, (n + 1) * width : (n + 2) * width] = columns


def scatter_kernel(capacity, stride, each, *refs):
    _, asked_ref, arrived_ref, hot_ref, cold_ref, mine_ref = refs
    devices = asked_ref.shape[0]
    hot_count, width = hot_ref.shape
    cold_count, cold_width = cold_ref.shape
    tiles = width // LANES
    asked = asked_ref[...].reshape(devices, LANES)
    stack = arrived_ref[...].astype(f32).reshape(devices, tiles * stride, LANES)
    stack = jnp.swapaxes(stack, 0, 1)
    rows, sums = [], []
    for n in range(tiles):
        part = stack[n * stride : n * stride + capacity]
        rows.append(part.reshape(capacity * devices, LANES).astype(low))
        sums.append(jnp.sum(stack[n * stride + capacity : n * stride + capacity + each], axis=1))
    rows = jnp.concatenate(rows, axis=1)
    hot_ref[...] = dot(asked_select(asked, capacity, 0, hot_count), rows, (0, 0))
    chosen = asked_select(asked, capacity, hot_count, cold_count)
    cold_ref[...] = dot(chosen, rows[:, :cold_width], (0, 0))
    mine_ref[...] = jnp.concatenate(sums, axis=1).astype(low)


def assemble(position, pieces, norm_scale, width):
    group, count = lax.axis_size("cp"), lax.axis_size("dp")
    share = width // group
    size = 5 * share // count
    if size % 16 == 0:
        return call(
            functools.partial(final_kernel, group, count, norm_scale),
            [position] + pieces,
            [shaped((width, 4 * width), f32), shaped((width, width), f32)],
            [pltpu.VMEM((group, count, size, width), low)],
        )
    result = jnp.zeros((group, count, size, width), low)
    for step, piece in zip(arrival_order(group), pieces):
        piece = piece.reshape(count, size, width)
        source = source_of(position[0], step, group)
        for n in range(count):
            place = (source, source_of(position[1], n, count), 0, 0)
            result = lax.dynamic_update_slice(result, piece[n][None, None], place)
    whole = result.reshape(group, count * size, width).astype(f32) * norm_scale
    output = whole[:, :share].reshape(width, width)
    gate = whole[:, share : 2 * share].reshape(width, width)
    rest = whole[:, 2 * share :].reshape(3 * width, width)
    return jnp.concatenate([gate, rest], axis=0).T, output


def local(
    row_owner,
    slot_row,
    hot_table,
    cold_table,
    cold_projection,
    joined_weight,
    output_weight,
    cotangent,
):
    tokens = slot_row.shape[0]
    width = output_weight.shape[0]
    hot_count = hot_table.shape[0]
    cold_count, cold_width = cold_table.shape
    head_size = width // HEADS
    score_scale = 1.0 / math.sqrt(head_size)
    everyone = ("dp", "cp")
    devices = lax.axis_size(everyone)
    group = lax.axis_size("cp")
    length = group * tokens
    position = jnp.stack([lax.axis_index("cp"), lax.axis_index("dp")]).astype(jnp.int32)
    capacity = 2 * tokens // devices + 2
    tiles = width // LANES
    each = cold_width // devices
    stride = capacity + each
    while tiles * stride % 8:
        stride += 1
    requests, rank, slot = call(
        request_kernel,
        [position, row_owner, slot_row[None, :]],
        [
            shaped((devices, 1, LANES), jnp.int32),
            shaped((tokens, 1), jnp.int32),
            shaped((tokens, 1), jnp.int32),
        ],
    )
    asked = lax.all_to_all(requests, everyone, split_axis=0, concat_axis=0, tiled=True)
    cotangents = gather_pieces(cotangent, "cp")
    near = (group + 1) // 2
    asked, *front = lax.optimization_barrier((asked, *cotangents[:near]))
    cotangents = front + cotangents[near:]
    picked = call(
        functools.partial(pick_kernel, capacity),
        [position, asked, hot_table, cold_table],
        [shaped((devices * tiles * capacity, LANES), low)],
    )[0]
    rows_back = lax.all_to_all(
        picked.reshape(devices, tiles * capacity, LANES),
        everyone,
        split_axis=0,
        concat_axis=0,
        tiled=True,
    ).reshape(picked.shape)
    vector, embedded, normed_low = call(
        functools.partial(embed_kernel, capacity, hot_count),
        [position, row_owner, rank, slot, rows_back, cold_projection],
        [
            shaped((tokens, cold_width), low),
            shaped((tokens, width), f32),
            shaped((tokens, width), low),
        ],
    )
    normed_low, *cotangents = lax.optimization_barrier((normed_low, *cotangents))
    hidden, active = call(
        hidden_kernel,
        [position, normed_low, joined_weight],
        [shaped((tokens, 4 * width), f32), shaped((tokens, 4 * width), low)],
        flops=8 * tokens * width * width,
    )
    normeds = gather_pieces(normed_low, "cp")
    share = width // group
    work = 2 * tokens * length * width
    mask = pltpu.VMEM((tokens, length), f32)
    layer_out, delta_attended, gate_hidden, early, everything = call(
        functools.partial(forward_kernel, group, score_scale, head_size),
        [position, *normeds, joined_weight, active, hidden, embedded, output_weight, cotangent],
        [
            shaped((tokens, width), low),
            shaped((tokens, width), low),
            shaped((tokens, width), low),
            shaped((group, 2 * share, tokens), low),
            shaped((length, 2 * width), low),
        ],
        [pltpu.VMEM((group, tokens, width), low), mask, pltpu.VMEM((tokens, width), f32)],
        2 * work + 4 * length * width * width,
    )
    query_hidden, all_queries = call(
        functools.partial(query_kernel, group, score_scale, head_size),
        [position, *normeds, joined_weight, active, everything, delta_attended, hidden],
        [shaped((tokens, width), low), shaped((length, width), low)],
        [pltpu.VMEM((group, tokens, width), low), mask],
        3 * work,
    )
    deltas = gather_pieces(delta_attended, "cp")
    rest_hidden, columns = call(
        functools.partial(key_kernel, group, score_scale, head_size),
        [position, *deltas, active, all_queries, hidden, query_hidden, early],
        [shaped((tokens, 3 * width), low), shaped((group, 5 * share, tokens), low)],
        [pltpu.VMEM((length, width), low), mask],
        4 * work,
    )
    moved = lax.all_to_all(columns, "cp", split_axis=0, concat_axis=0, tiled=True)
    sent = call(
        functools.partial(row_kernel, hot_count, capacity, stride),
        [
            position,
            gate_hidden,
            rest_hidden,
            joined_weight,
            embedded,
            cotangent,
            vector,
            row_owner,
            rank,
            slot,
            cold_projection,
        ],
        [shaped((devices * tiles * stride, LANES), low)],
        flops=8 * tokens * width * width,
        limit=56,
    )[0]
    sent = sent.reshape(devices, tiles * stride, LANES)
    arrived = lax.all_to_all(sent, everyone, split_axis=0, concat_axis=0, tiled=True)
    count = lax.axis_size("dp")
    chunk = 5 * share // count
    own, *sends = call(
        functools.partial(weight_kernel, group, count),
        [position, moved, *cotangents, *normeds],
        [shaped((chunk, width), f32)] + [shaped((chunk, width), low)] * (count - 1),
        [pltpu.VMEM((count, chunk, width), f32)],
        10 * share * length * width,
        limit=56,
    )
    for step, block in enumerate(sends, start=1):
        own = own + exchange(block, "dp", step).astype(f32)
    mine = own.astype(low)
    line = [mine] + [exchange(mine, "dp", step) for step in range(1, count)]
    line = jnp.concatenate(line, axis=0)
    hot_gradient, cold_gradient, total = call(
        functools.partial(scatter_kernel, capacity, stride, each),
        [position, asked, arrived.reshape(devices * tiles * stride, LANES)],
        [
            shaped((hot_count, width), f32),
            shaped((cold_count, cold_width), f32),
            shaped((each, width), low),
        ],
        flops=4 * devices * capacity * hot_count * width,
        limit=56,
    )
    copies = jnp.broadcast_to(total[None], (devices, each, width))
    projection = lax.all_to_all(copies, everyone, split_axis=0, concat_axis=0, tiled=True)
    pieces = gather_pieces(line, "cp", (projection, hot_gradient, cold_gradient))
    norm_scale = (tokens * devices) ** (-0.5)
    joined_gradient, output_gradient = assemble(position, pieces, norm_scale, width)
    return (
        layer_out,
        hot_gradient,
        cold_gradient,
        projection.reshape(cold_width, width).astype(f32) * norm_scale,
        joined_gradient,
        output_gradient,
    )


def solution(mesh):
    placed = (
        P(("dp", "cp"), None),
        P(("dp", "cp")),
        P(("dp", "cp"), None),
        P(("dp", "cp"), None),
        P(),
        P(),
        P(),
        P(("dp", "cp"), None),
    )
    return jax.shard_map(
        local,
        mesh=mesh,
        in_specs=placed,
        out_specs=(
            P(("dp", "cp"), None),
            P(("dp", "cp"), None),
            P(("dp", "cp"), None),
            P(),
            P(),
            P(),
        ),
        check_vma=False,
    )
```

```python
import functools
import math

import jax
import jax.numpy as jnp
from jax import lax
from jax.experimental import pallas as pl
from jax.experimental.pallas import tpu as pltpu
from jax.sharding import PartitionSpec as P


HEADS = 8
LANES = 128


EPSILON = 1e-05
low = jnp.bfloat16
f32 = jnp.float32
SMEM = pl.BlockSpec(memory_space=pltpu.SMEM)
VMEM = pl.BlockSpec(memory_space=pltpu.VMEM)


def sigmoid(values):
    return 0.5 + 0.5 * jnp.tanh(0.5 * values)


def silu(values):
    return values * sigmoid(values)


def silu_slope(values):
    sigmoid_v = sigmoid(values)
    return sigmoid_v * (1.0 + values * (1.0 - sigmoid_v))


def layer_normalize(values):
    average = jnp.mean(values, axis=-1, keepdims=True)
    centred = values - average
    inverse = lax.rsqrt(jnp.mean(centred * centred, axis=-1, keepdims=True) + EPSILON)
    return (centred * inverse, inverse)


def normalize_back(gradient, normed, inverse):
    first_term = jnp.mean(gradient, axis=-1, keepdims=True)
    second_term = jnp.mean(gradient * normed, axis=-1, keepdims=True)
    return (gradient - first_term - normed * second_term) * inverse


def dot(left, right, contract=(1, 0)):
    dims = (((contract[0],), (contract[1],)), ((), ()))
    return lax.dot_general(left, right, dims, preferred_element_type=f32)


def power_of_two(count):
    return count & (count - 1) == 0


def source_of(here, step, count):
    if power_of_two(count):
        return here ^ step
    return (here + count - step) % count


def target_of(here, step, count):
    if power_of_two(count):
        return here ^ step
    return (here + step) % count


def exchange(block, axis, step):
    count = lax.axis_size(axis)
    pairs = [(i, target_of(i, step, count)) for i in range(count)]
    return lax.ppermute(block, axis, pairs)


def arrival_order(count):
    if not power_of_two(count) or count < 4:
        return list(range(count))
    return list(range(0, count, 2)) + list(range(1, count, 2))


def gather_pieces(block, axis, after=None):
    count = lax.axis_size(axis)
    if not power_of_two(count) or count < 4:
        return [block] + [exchange(block, axis, step) for step in range(1, count)]
    near = [block]
    for step in range(2, count, 2):
        near.append(exchange(block, axis, step))
    if after is not None:
        near = list(lax.optimization_barrier((*near, *after))[: len(near)])
    return near + [exchange(piece, axis, 1) for piece in near]


def call(kernel, operands, outs, scratch=(), flops=0, scalars=1, limit=24):
    moved = sum(x.size * x.dtype.itemsize for x in list(operands) + list(outs))
    return pl.pallas_call(
        kernel,
        out_shape=outs,
        in_specs=[SMEM] * scalars + [VMEM] * (len(operands) - scalars),
        out_specs=[VMEM] * len(outs),
        scratch_shapes=list(scratch),
        cost_estimate=pl.CostEstimate(flops=flops, bytes_accessed=moved, transcendentals=0),
        compiler_params=pltpu.CompilerParams(vmem_limit_bytes=limit << 20),
    )(*operands)


def shaped(shape, dtype):
    return jax.ShapeDtypeStruct(shape, dtype)


def tile(index, size=LANES):
    return pl.ds(pl.multiple_of(index * size, size), size)


def head_masks(rows, head_size):
    lane = lax.broadcasted_iota(jnp.int32, (rows, LANES), 1)
    return [lane // head_size == n for n in range(LANES // head_size)]


def only(mask, values):
    return jnp.where(mask, values, jnp.zeros((), values.dtype))


def merge(masks, parts):
    result = parts[-1]
    for mask, part in zip(masks[:-1], parts[:-1]):
        result = jnp.where(mask, part, result)
    return result


def fill_mask(mask_ref, here, order, group, tokens, forward):
    row = lax.broadcasted_iota(jnp.int32, (tokens, tokens), 0)
    column = lax.broadcasted_iota(jnp.int32, (tokens, tokens), 1)
    for n, step in enumerate(order):
        gap = (here - source_of(here, step, group)) * tokens
        allowed = (column - row <= gap) if forward else (column - row >= gap)
        mask_ref[:, n * tokens : (n + 1) * tokens] = allowed.astype(f32)


def unit_mask(size):
    row = lax.broadcasted_iota(jnp.int32, (size, size), 0)
    return row == lax.broadcasted_iota(jnp.int32, (size, size), 1)


def as_row(column):
    return jnp.sum(jnp.where(unit_mask(column.shape[0]), column, 0), axis=0, keepdims=True)


def as_column(row):
    return jnp.sum(jnp.where(unit_mask(row.shape[1]), row, 0), axis=1, keepdims=True)


def selected(flags):
    return flags.astype(f32).astype(low)


def request_kernel(here_ref, owner_ref, slot_ref, request_ref, rank_ref, column_ref, owners_ref):
    tokens = owner_ref.shape[1]
    devices = request_ref.shape[0]
    owners = as_column(owner_ref[...])
    owners_ref[...] = owners
    named = owners == lax.broadcasted_iota(jnp.int32, (tokens, devices), 1)
    row = lax.broadcasted_iota(jnp.int32, (tokens, tokens), 0)
    lower = selected(row > lax.broadcasted_iota(jnp.int32, (tokens, tokens), 1))
    earlier = dot(lower, selected(named))
    rank = jnp.sum(jnp.where(named, earlier, 0.0), axis=1, keepdims=True).astype(jnp.int32)
    rank_ref[...] = rank
    slot = as_column(slot_ref[...])
    column_ref[...] = slot
    ranked = rank == lax.broadcasted_iota(jnp.int32, (tokens, LANES), 1)
    code = slot + 1
    high = jnp.where(ranked, code >> 6, 0).astype(f32).astype(low)
    rest = jnp.where(ranked, code & 63, 0).astype(f32).astype(low)
    names = selected(named)
    total = dot(names, high, (0, 0)) * 64.0 + dot(names, rest, (0, 0)) - 1.0
    request_ref[...] = total.astype(jnp.int32).reshape(devices, 1, LANES)


def asked_select(asked, capacity, first, count):
    index = lax.broadcasted_iota(jnp.int32, (asked.shape[0], count), 1) + first
    parts = [selected(asked[:, n : n + 1] == index) for n in range(capacity)]
    return jnp.concatenate(parts, axis=0)


def pick_kernel(capacity, here_ref, asked_ref, hot_ref, cold_ref, out_ref):
    devices = asked_ref.shape[0]
    hot_count, width = hot_ref.shape
    cold_count, cold_width = cold_ref.shape
    asked = asked_ref[...].reshape(devices, LANES)
    hot = dot(asked_select(asked, capacity, 0, hot_count), hot_ref[...])
    cold = dot(asked_select(asked, capacity, hot_count, cold_count), cold_ref[...])
    tiles = [hot[:, n * LANES : (n + 1) * LANES] for n in range(width // LANES)]
    for n in range(cold_width // LANES):
        tiles[n] = tiles[n] + cold[:, n * LANES : (n + 1) * LANES]
    stack = jnp.concatenate(tiles, axis=0).reshape(len(tiles) * capacity, devices, LANES)
    out_ref[...] = jnp.swapaxes(stack, 0, 1).reshape(out_ref.shape).astype(low)


def embed_kernel(capacity, hot_count, *refs):
    _, owner_ref, rank_ref, slot_ref, rows_ref, cold_ref = refs[:6]
    vector_ref, embedded_ref, normed_ref = refs[6:]
    tokens, width = embedded_ref.shape
    cold_width = cold_ref.shape[0]
    tiles = width // LANES
    base = owner_ref[...] * (tiles * capacity) + rank_ref[...]
    index = lax.broadcasted_iota(jnp.int32, (tokens, rows_ref.shape[0]), 1)
    parts = [
        dot(selected(index == base + n * capacity), rows_ref[...]) for n in range(tiles)
    ]
    vector = jnp.concatenate(parts, axis=1)
    narrow = vector[:, :cold_width].astype(low)
    vector_ref[...] = narrow
    embedded = jnp.where(slot_ref[...] >= hot_count, dot(narrow, cold_ref[...]), vector)
    embedded_ref[...] = embedded
    normed_ref[...] = layer_normalize(embedded)[0].astype(low)


def hidden_kernel(here_ref, normed_ref, weight_ref, hidden_ref, active_ref):
    hidden = dot(normed_ref[...], weight_ref[...])
    hidden_ref[...] = hidden
    active_ref[...] = silu(hidden).astype(low)


def forward_kernel(group, scale, head_size, *refs):
    here_ref, pieces = refs[0], refs[1 : 1 + group]
    weight_ref, active_ref, hidden_ref, mix_ref, cotangent_ref = refs[1 + group : 6 + group]
    gated_ref, delta_ref, gate_ref, early_ref, all_ref, normed_scr, mask_scr, att_scr = refs[6 + group :]
    tokens, width = cotangent_ref.shape
    order = arrival_order(group)
    here = here_ref[0]
    for n in range(1, group):
        normed_scr[n] = pieces[n][...]
    fill_mask(mask_scr, here, order, group, tokens, True)
    all_ref[0:tokens, :width] = active_ref[:, width : 2 * width]
    all_ref[0:tokens, width:] = active_ref[:, 3 * width :]

    def project(n, carry):
        hidden = dot(normed_scr[n], weight_ref[:, width : 2 * width])
        all_ref[tile(n, tokens), :width] = silu(hidden).astype(low)
        hidden = dot(normed_scr[n], weight_ref[:, 3 * width :])
        all_ref[tile(n, tokens), width:] = silu(hidden).astype(low)
        return carry

    lax.fori_loop(1, group, project, 0)
    masks = head_masks(tokens, head_size)

    def attend(n, carry):
        values = all_ref[:, tile(n)]
        queries = active_ref[:, tile(n + 2 * width // LANES)]
        keys = all_ref[:, tile(n + width // LANES)]
        parts = []
        for mask in masks:
            scores = dot(only(mask, queries), keys, (1, 1)) * scale
            weights = (silu(scores) * mask_scr[...]).astype(low)
            parts.append(dot(weights, values))
        att_scr[:, tile(n)] = merge(masks, parts)
        return carry

    lax.fori_loop(0, width // LANES, attend, 0, unroll=True)
    mixed, inverse_mix = layer_normalize(att_scr[...])
    gate = active_ref[:, :width].astype(f32)
    gated = (mixed * gate).astype(low)
    gated_ref[...] = gated
    delta_gated = dot(cotangent_ref[...], mix_ref[...], (1, 1))
    delta_ref[...] = normalize_back(delta_gated * gate, mixed, inverse_mix).astype(low)
    gate_hidden = (delta_gated * mixed * silu_slope(hidden_ref[:, :width])).astype(low)
    gate_ref[...] = gate_hidden
    share = width // group
    gated_t = gated.astype(f32).T.astype(low)
    hidden_t = gate_hidden.astype(f32).T.astype(low)
    for n in range(group):
        early_ref[n, 0:share] = gated_t[n * share : (n + 1) * share]
        early_ref[n, share : 2 * share] = hidden_t[n * share : (n + 1) * share]


def out_kernel(here_ref, gated_ref, mix_ref, embedded_ref, out_ref):
    out_ref[...] = (embedded_ref[...] + dot(gated_ref[...], mix_ref[...])).astype(low)


def query_kernel(group, scale, head_size, *refs):
    here_ref, pieces = refs[0], refs[1 : 1 + group]
    weight_ref, active_ref, all_ref, delta_ref, hidden_ref = refs[1 + group : 6 + group]
    out_ref, queries_ref, normed_scr, mask_scr = refs[6 + group :]
    tokens, width = delta_ref.shape
    for n in range(1, group):
        normed_scr[n] = pieces[n][...]
    queries_ref[0:tokens, :] = active_ref[:, 2 * width : 3 * width]

    def project(n, carry):
        hidden = dot(normed_scr[n], weight_ref[:, 2 * width : 3 * width])
        queries_ref[tile(n, tokens), :] = silu(hidden).astype(low)
        return carry

    lax.fori_loop(1, group, project, 0)
    fill_mask(mask_scr, here_ref[0], arrival_order(group), group, tokens, True)
    masks = head_masks(tokens, head_size)

    def step(n, carry):
        values = all_ref[:, tile(n)]
        queries = active_ref[:, tile(n + 2 * width // LANES)]
        keys = all_ref[:, tile(n + width // LANES)]
        delta = delta_ref[:, tile(n)]
        parts = []
        for mask in masks:
            scores = dot(only(mask, queries), keys, (1, 1)) * scale
            change = dot(only(mask, delta), values, (1, 1))
            change = (change * silu_slope(scores) * (mask_scr[...] * scale)).astype(low)
            parts.append(dot(change, keys))
        slope = silu_slope(hidden_ref[:, tile(n + 2 * width // LANES)])
        out_ref[:, tile(n)] = (merge(masks, parts) * slope).astype(low)
        return carry

    lax.fori_loop(0, width // LANES, step, 0, unroll=True)


def key_kernel(group, scale, head_size, *refs):
    here_ref, pieces = refs[0], refs[1 : 1 + group]
    active_ref, queries_ref, hidden_ref, query_ref, early_ref = refs[1 + group : 6 + group]
    rest_ref, columns = refs[6 + group], refs[7 + group : 7 + 2 * group]
    column_scr, delta_scr, mask_scr = refs[7 + 2 * group :]
    tokens, width = query_ref.shape
    for n in range(group):
        delta_scr[n * tokens : (n + 1) * tokens, :] = pieces[n][...]
    fill_mask(mask_scr, here_ref[0], arrival_order(group), group, tokens, False)
    masks = head_masks(tokens, head_size)
    tiles = width // LANES

    def step(n, carry):
        values = active_ref[:, tile(n + tiles)]
        queries = queries_ref[:, tile(n)]
        keys = active_ref[:, tile(n + 3 * tiles)]
        delta = delta_scr[:, tile(n)]
        value_parts, key_parts = [], []
        for mask in masks:
            scores = dot(only(mask, keys), queries, (1, 1)) * scale
            change = dot(only(mask, values), delta, (1, 1))
            sigmoid_v = sigmoid(scores)
            weights = (scores * sigmoid_v * mask_scr[...]).astype(low)
            slope = sigmoid_v * (1.0 + scores * (1.0 - sigmoid_v))
            change = (change * slope * (mask_scr[...] * scale)).astype(low)
            value_parts.append(dot(weights, delta))
            key_parts.append(dot(change, queries))
        for parts, at in ((value_parts, 0), (key_parts, 2)):
            slope = silu_slope(hidden_ref[:, tile(n + (at + 1) * tiles)])
            rest_ref[:, tile(n + at * tiles)] = (merge(masks, parts) * slope).astype(low)
        return carry

    lax.fori_loop(0, tiles, step, 0, unroll=True)
    rest_ref[:, width : 2 * width] = query_ref[...]
    late = rest_ref[...].astype(f32).T.astype(low)
    share = width // group
    for n in range(group):
        column_scr[n, : 2 * share] = early_ref[n]
        column_scr[n, 2 * share :] = late[3 * n * share : 3 * (n + 1) * share]
    for n, step in enumerate(arrival_order(group)):
        columns[n][...] = column_scr[target_of(here_ref[0], step, group)]


def row_kernel(head_rows, capacity, stride, *refs):
    _, gate_ref, rest_ref, weight_ref, embedded_ref, cotangent_ref = refs[:6]
    vector_ref, owner_ref, rank_ref, slot_ref, cold_ref, sent_ref = refs[6:]
    _, width = embedded_ref.shape
    cold_width = cold_ref.shape[0]
    tiles = width // LANES
    devices = sent_ref.shape[0] // (tiles * stride)
    delta_normed = dot(gate_ref[...], weight_ref[:, :width], (1, 1))
    delta_normed += dot(rest_ref[...], weight_ref[:, width:], (1, 1))
    normed, inverse = layer_normalize(embedded_ref[...])
    delta_embed = normalize_back(delta_normed, normed, inverse) + cotangent_ref[...].astype(f32)
    delta_low = delta_embed.astype(low)
    cold = slot_ref[...] >= head_rows
    cold_event = dot(delta_low, cold_ref[...], (1, 1))
    hot_event = jnp.where(cold, 0.0, delta_embed)
    narrow = jnp.where(cold, cold_event, hot_event[:, :cold_width])
    event = jnp.concatenate([narrow, hot_event[:, cold_width:]], axis=1).astype(low)
    cold_rows = jnp.where(cold, vector_ref[...].astype(f32), 0.0).astype(low)
    part = dot(cold_rows, delta_low, (0, 0)).astype(low)
    each = cold_width // devices
    row = lax.broadcasted_iota(jnp.int32, (1, cold_width), 1)
    own = (row // each) * (tiles * stride) + capacity + row % each
    place = as_row(owner_ref[...] * (tiles * stride) + rank_ref[...])
    place = jnp.concatenate([place, own], axis=1)
    both = jnp.concatenate([event, part], axis=0)
    index = lax.broadcasted_iota(jnp.int32, (sent_ref.shape[0], place.shape[1]), 0)
    total = None
    for n in range(tiles):
        chosen = selected(index == place + n * stride)
        term = dot(chosen, both[:, n * LANES : (n + 1) * LANES])
        total = term if n == 0 else total + term
    sent_ref[...] = total.astype(low)


def weight_kernel(group, count, *refs):
    here_ref, moved = refs[0], refs[1 : 1 + group]
    cotangents, normeds = refs[1 + group : 1 + 2 * group], refs[1 + 2 * group : 1 + 3 * group]
    own_ref = refs[1 + 3 * group]
    sends = refs[2 + 3 * group : 1 + 3 * group + count]
    part_scr = refs[1 + 3 * group + count]
    outer = here_ref[1]
    share = moved[0].shape[0] // 5
    chunk = own_ref.shape[0]
    top = bottom = None
    for n in range(group):
        first = dot(moved[n][:share], cotangents[n][...])
        second = dot(moved[n][share:], normeds[n][...])
        top = first if n == 0 else top + first
        bottom = second if n == 0 else bottom + second
    total = jnp.concatenate([top, bottom], axis=0)
    for n in range(count):
        part_scr[n] = total[n * chunk : (n + 1) * chunk]
    own_ref[...] = part_scr[outer]
    for step in range(1, count):
        sends[step - 1][...] = part_scr[target_of(outer, step, count)].astype(low)


def final_kernel(group, count, norm_scale, *refs):
    here_ref, pieces = refs[0], refs[1 : 1 + group]
    joined_ref, output_ref, piece_scr = refs[1 + group :]
    here, outer = here_ref[0], here_ref[1]
    width = output_ref.shape[0]
    chunk = piece_scr.shape[2]
    for n, step in enumerate(arrival_order(group)):
        source = source_of(here, step, group)
        for m in range(count):
            part = pieces[n][m * chunk : (m + 1) * chunk]
            piece_scr[source, source_of(outer, m, count)] = part
    share = width // group
    row = lax.broadcasted_iota(jnp.int32, (width, width), 0)
    column = lax.broadcasted_iota(jnp.int32, (width, width), 1)
    unit = (row == column).astype(f32).astype(low)
    blocks = [piece_scr[n].reshape(5 * share, width) for n in range(group)]
    for n in range(group):
        output_ref[n * share : (n + 1) * share, :] = blocks[n][:share].astype(f32) * norm_scale
    gate = jnp.concatenate([block[share : 2 * share] for block in blocks], axis=0)
    joined_ref[:, :width] = dot(unit, gate, (1, 1)) * norm_scale
    rest = jnp.concatenate([block[2 * share :] for block in blocks], axis=0)
    for n in range(3):
        columns = dot(unit, rest[n * width : (n + 1) * width], (1, 1)) * norm_scale
        joined_ref[:, (n + 1) * width : (n + 2) * width] = columns


def scatter_kernel(capacity, stride, each, *refs):
    _, asked_ref, arrived_ref, hot_ref, cold_ref, mine_ref = refs
    devices = asked_ref.shape[0]
    hot_count, width = hot_ref.shape
    cold_count, cold_width = cold_ref.shape
    tiles = width // LANES
    asked = asked_ref[...].reshape(devices, LANES)
    stack = arrived_ref[...].astype(f32).reshape(devices, tiles * stride, LANES)
    stack = jnp.swapaxes(stack, 0, 1)
    rows, sums = [], []
    for n in range(tiles):
        part = stack[n * stride : n * stride + capacity]
        rows.append(part.reshape(capacity * devices, LANES).astype(low))
        sums.append(jnp.sum(stack[n * stride + capacity : n * stride + capacity + each], axis=1))
    rows = jnp.concatenate(rows, axis=1)
    hot_ref[...] = dot(asked_select(asked, capacity, 0, hot_count), rows, (0, 0))
    chosen = asked_select(asked, capacity, hot_count, cold_count)
    cold_ref[...] = dot(chosen, rows[:, :cold_width], (0, 0))
    mine_ref[...] = jnp.broadcast_to(jnp.concatenate(sums, axis=1)[None], mine_ref.shape).astype(low)


def assemble(position, pieces, norm_scale, width):
    group, count = lax.axis_size("cp"), lax.axis_size("dp")
    share = width // group
    size = 5 * share // count
    if size % 16 == 0:
        return call(
            functools.partial(final_kernel, group, count, norm_scale),
            [position] + pieces,
            [shaped((width, 4 * width), f32), shaped((width, width), f32)],
            [pltpu.VMEM((group, count, size, width), low)],
        )
    result = jnp.zeros((group, count, size, width), low)
    for step, piece in zip(arrival_order(group), pieces):
        piece = piece.reshape(count, size, width)
        source = source_of(position[0], step, group)
        for n in range(count):
            place = (source, source_of(position[1], n, count), 0, 0)
            result = lax.dynamic_update_slice(result, piece[n][None, None], place)
    whole = result.reshape(group, count * size, width).astype(f32) * norm_scale
    output = whole[:, :share].reshape(width, width)
    gate = whole[:, share : 2 * share].reshape(width, width)
    rest = whole[:, 2 * share :].reshape(3 * width, width)
    return jnp.concatenate([gate, rest], axis=0).T, output


def local(
    row_owner,
    slot_row,
    hot_table,
    cold_table,
    cold_projection,
    joined_weight,
    output_weight,
    cotangent,
):
    tokens = slot_row.shape[0]
    width = output_weight.shape[0]
    hot_count = hot_table.shape[0]
    cold_count, cold_width = cold_table.shape
    head_size = width // HEADS
    score_scale = 1.0 / math.sqrt(head_size)
    everyone = ("dp", "cp")
    devices = lax.axis_size(everyone)
    group = lax.axis_size("cp")
    length = group * tokens
    position = jnp.stack([lax.axis_index("cp"), lax.axis_index("dp")]).astype(jnp.int32)
    capacity = 2 * tokens // devices + 2
    tiles = width // LANES
    each = cold_width // devices
    stride = capacity + each
    while tiles * stride % 8:
        stride += 1
    requests, rank, slot, owners = call(
        request_kernel,
        [position, row_owner.reshape(1, tokens), slot_row[None, :]],
        [
            shaped((devices, 1, LANES), jnp.int32),
            shaped((tokens, 1), jnp.int32),
            shaped((tokens, 1), jnp.int32),
            shaped((tokens, 1), jnp.int32),
        ],
    )
    asked = lax.all_to_all(requests, everyone, split_axis=0, concat_axis=0, tiled=True)
    cotangents = gather_pieces(cotangent, "cp")
    near = (group + 1) // 2
    asked, *front = lax.optimization_barrier((asked, *cotangents[:near]))
    cotangents = front + cotangents[near:]
    picked = call(
        functools.partial(pick_kernel, capacity),
        [position, asked, hot_table, cold_table],
        [shaped((devices * tiles * capacity, LANES), low)],
        limit=56,
    )[0]
    rows_back = lax.all_to_all(
        picked.reshape(devices, tiles * capacity, LANES),
        everyone,
        split_axis=0,
        concat_axis=0,
        tiled=True,
    ).reshape(picked.shape)
    vector, embedded, normed_low = call(
        functools.partial(embed_kernel, capacity, hot_count),
        [position, owners, rank, slot, rows_back, cold_projection],
        [
            shaped((tokens, cold_width), low),
            shaped((tokens, width), f32),
            shaped((tokens, width), low),
        ],
    )
    normed_low, *cotangents = lax.optimization_barrier((normed_low, *cotangents))
    hidden, active = call(
        hidden_kernel,
        [position, normed_low, joined_weight],
        [shaped((tokens, 4 * width), f32), shaped((tokens, 4 * width), low)],
        flops=8 * tokens * width * width,
    )
    normeds = gather_pieces(normed_low, "cp")
    share = width // group
    work = 2 * tokens * length * width
    mask = pltpu.VMEM((tokens, length), f32)
    gated, delta_attended, gate_hidden, early, everything = call(
        functools.partial(forward_kernel, group, score_scale, head_size),
        [position, *normeds, joined_weight, active, hidden, output_weight, cotangent],
        [
            shaped((tokens, width), low),
            shaped((tokens, width), low),
            shaped((tokens, width), low),
            shaped((group, 2 * share, tokens), low),
            shaped((length, 2 * width), low),
        ],
        [pltpu.VMEM((group, tokens, width), low), mask, pltpu.VMEM((tokens, width), f32)],
        2 * work + 4 * length * width * width,
    )
    query_hidden, all_queries = call(
        functools.partial(query_kernel, group, score_scale, head_size),
        [position, *normeds, joined_weight, active, everything, delta_attended, hidden],
        [shaped((tokens, width), low), shaped((length, width), low)],
        [pltpu.VMEM((group, tokens, width), low), mask],
        3 * work,
    )
    deltas = gather_pieces(delta_attended, "cp")
    rest_hidden, *columns = call(
        functools.partial(key_kernel, group, score_scale, head_size),
        [position, *deltas, active, all_queries, hidden, query_hidden, early],
        [shaped((tokens, 3 * width), low)] + [shaped((5 * share, tokens), low)] * group,
        [pltpu.VMEM((group, 5 * share, tokens), low), pltpu.VMEM((length, width), low), mask],
        4 * work,
    )
    moved = columns[:1]
    for step, block in zip(arrival_order(group)[1:], columns[1:]):
        moved.append(exchange(block, "cp", step))
    sent = call(
        functools.partial(row_kernel, hot_count, capacity, stride),
        [
            position,
            gate_hidden,
            rest_hidden,
            joined_weight,
            embedded,
            cotangent,
            vector,
            owners,
            rank,
            slot,
            cold_projection,
        ],
        [shaped((devices * tiles * stride, LANES), low)],
        flops=8 * tokens * width * width,
        limit=56,
    )[0]
    sent = sent.reshape(devices, tiles * stride, LANES)
    arrived = lax.all_to_all(sent, everyone, split_axis=0, concat_axis=0, tiled=True)
    layer_out = call(
        out_kernel,
        [position, gated, output_weight, embedded],
        [shaped((tokens, width), low)],
        limit=56,
    )[0]
    count = lax.axis_size("dp")
    chunk = 5 * share // count
    own, *sends = call(
        functools.partial(weight_kernel, group, count),
        [position, *moved, *cotangents, *normeds],
        [shaped((chunk, width), f32)] + [shaped((chunk, width), low)] * (count - 1),
        [pltpu.VMEM((count, chunk, width), f32)],
        10 * share * length * width,
        limit=56,
    )
    for step, block in enumerate(sends, start=1):
        block = exchange(block, "dp", step)
        own = own + block.astype(f32)
    mine = own.astype(low)
    line = [mine]
    for step in range(1, count):
        line.append(exchange(mine, "dp", step))
    line = jnp.concatenate(line, axis=0)
    hot_gradient, cold_gradient, copies = call(
        functools.partial(scatter_kernel, capacity, stride, each),
        [position, asked, arrived.reshape(devices * tiles * stride, LANES)],
        [
            shaped((hot_count, width), f32),
            shaped((cold_count, cold_width), f32),
            shaped((devices, each, width), low),
        ],
        flops=4 * devices * capacity * hot_count * width,
        limit=56,
    )
    projection = lax.all_to_all(copies, everyone, split_axis=0, concat_axis=0, tiled=True)
    pieces = gather_pieces(line, "cp", (projection, hot_gradient, cold_gradient))
    norm_scale = (tokens * devices) ** (-0.5)
    joined_gradient, output_gradient = assemble(position, pieces, norm_scale, width)
    return (
        layer_out,
        hot_gradient,
        cold_gradient,
        projection.reshape(cold_width, width).astype(f32) * norm_scale,
        joined_gradient,
        output_gradient,
    )


def solution(mesh):
    placed = (
        P(("dp", "cp"), None),
        P(("dp", "cp")),
        P(("dp", "cp"), None),
        P(("dp", "cp"), None),
        P(),
        P(),
        P(),
        P(("dp", "cp"), None),
    )
    return jax.shard_map(
        local,
        mesh=mesh,
        in_specs=placed,
        out_specs=(
            P(("dp", "cp"), None),
            P(("dp", "cp"), None),
            P(("dp", "cp"), None),
            P(),
            P(),
            P(),
        ),
        check_vma=False,
    )
```

```python
import functools
import math

import jax
import jax.numpy as jnp
from jax import lax
from jax.experimental import pallas as pl
from jax.experimental.pallas import tpu as pltpu
from jax.sharding import PartitionSpec as P


HEADS = 8
LANES = 128


EPSILON = 1e-05
low = jnp.bfloat16
f32 = jnp.float32
SMEM = pl.BlockSpec(memory_space=pltpu.SMEM)
VMEM = pl.BlockSpec(memory_space=pltpu.VMEM)


def sigmoid(values):
    return 0.5 + 0.5 * jnp.tanh(0.5 * values)


def silu(values):
    return values * sigmoid(values)


def silu_slope(values):
    sigmoid_v = sigmoid(values)
    return sigmoid_v * (1.0 + values * (1.0 - sigmoid_v))


def layer_normalize(values):
    average = jnp.mean(values, axis=-1, keepdims=True)
    centred = values - average
    inverse = lax.rsqrt(jnp.mean(centred * centred, axis=-1, keepdims=True) + EPSILON)
    return (centred * inverse, inverse)


def normalize_back(gradient, normed, inverse):
    first_term = jnp.mean(gradient, axis=-1, keepdims=True)
    second_term = jnp.mean(gradient * normed, axis=-1, keepdims=True)
    return (gradient - first_term - normed * second_term) * inverse


def dot(left, right, contract=(1, 0)):
    dims = (((contract[0],), (contract[1],)), ((), ()))
    return lax.dot_general(left, right, dims, preferred_element_type=f32)


def power_of_two(count):
    return count & (count - 1) == 0


def source_of(here, step, count):
    if power_of_two(count):
        return here ^ step
    return (here + count - step) % count


def target_of(here, step, count):
    if power_of_two(count):
        return here ^ step
    return (here + step) % count


def exchange(block, axis, step):
    count = lax.axis_size(axis)
    pairs = [(i, target_of(i, step, count)) for i in range(count)]
    return lax.ppermute(block, axis, pairs)


def arrival_order(count):
    if not power_of_two(count) or count < 4:
        return list(range(count))
    return list(range(0, count, 2)) + list(range(1, count, 2))


def gather_pieces(block, axis, after=None):
    count = lax.axis_size(axis)
    if not power_of_two(count) or count < 4:
        return [block] + [exchange(block, axis, step) for step in range(1, count)]
    near = [block]
    for step in range(2, count, 2):
        near.append(exchange(block, axis, step))
    if after is not None:
        near = list(lax.optimization_barrier((*near, *after))[: len(near)])
    return near + [exchange(piece, axis, 1) for piece in near]


def call(kernel, operands, outs, scratch=(), flops=0, scalars=1, limit=24):
    moved = sum(x.size * x.dtype.itemsize for x in list(operands) + list(outs))
    return pl.pallas_call(
        kernel,
        out_shape=outs,
        in_specs=[SMEM] * scalars + [VMEM] * (len(operands) - scalars),
        out_specs=[VMEM] * len(outs),
        scratch_shapes=list(scratch),
        cost_estimate=pl.CostEstimate(flops=flops, bytes_accessed=moved, transcendentals=0),
        compiler_params=pltpu.CompilerParams(vmem_limit_bytes=limit << 20),
    )(*operands)


def shaped(shape, dtype):
    return jax.ShapeDtypeStruct(shape, dtype)


def tile(index, size=LANES):
    return pl.ds(pl.multiple_of(index * size, size), size)


def head_masks(rows, head_size):
    lane = lax.broadcasted_iota(jnp.int32, (rows, LANES), 1)
    return [lane // head_size == n for n in range(LANES // head_size)]


def only(mask, values):
    return jnp.where(mask, values, jnp.zeros((), values.dtype))


def merge(masks, parts):
    result = parts[-1]
    for mask, part in zip(masks[:-1], parts[:-1]):
        result = jnp.where(mask, part, result)
    return result


def fill_mask(mask_ref, here, order, group, tokens, forward):
    row = lax.broadcasted_iota(jnp.int32, (tokens, tokens), 0)
    column = lax.broadcasted_iota(jnp.int32, (tokens, tokens), 1)
    for n, step in enumerate(order):
        gap = (here - source_of(here, step, group)) * tokens
        allowed = (column - row <= gap) if forward else (column - row >= gap)
        mask_ref[:, n * tokens : (n + 1) * tokens] = allowed.astype(f32)


def unit_mask(size):
    row = lax.broadcasted_iota(jnp.int32, (size, size), 0)
    return row == lax.broadcasted_iota(jnp.int32, (size, size), 1)


def as_row(column):
    return jnp.sum(jnp.where(unit_mask(column.shape[0]), column, 0), axis=0, keepdims=True)


def as_column(row):
    return jnp.sum(jnp.where(unit_mask(row.shape[1]), row, 0), axis=1, keepdims=True)


def selected(flags):
    return flags.astype(f32).astype(low)


def request_kernel(here_ref, owner_ref, slot_ref, request_ref, rank_ref, column_ref, owners_ref):
    tokens = owner_ref.shape[1]
    devices = request_ref.shape[0]
    owners = as_column(owner_ref[...])
    owners_ref[...] = owners
    named = owners == lax.broadcasted_iota(jnp.int32, (tokens, devices), 1)
    row = lax.broadcasted_iota(jnp.int32, (tokens, tokens), 0)
    lower = selected(row > lax.broadcasted_iota(jnp.int32, (tokens, tokens), 1))
    earlier = dot(lower, selected(named))
    rank = jnp.sum(jnp.where(named, earlier, 0.0), axis=1, keepdims=True).astype(jnp.int32)
    rank_ref[...] = rank
    slot = as_column(slot_ref[...])
    column_ref[...] = slot
    ranked = rank == lax.broadcasted_iota(jnp.int32, (tokens, LANES), 1)
    code = slot + 1
    high = jnp.where(ranked, code >> 6, 0).astype(f32).astype(low)
    rest = jnp.where(ranked, code & 63, 0).astype(f32).astype(low)
    names = selected(named)
    total = dot(names, high, (0, 0)) * 64.0 + dot(names, rest, (0, 0)) - 1.0
    request_ref[...] = total.astype(jnp.int32).reshape(devices, 1, LANES)


def asked_select(asked, capacity, first, count):
    index = lax.broadcasted_iota(jnp.int32, (asked.shape[0], count), 1) + first
    parts = [selected(asked[:, n : n + 1] == index) for n in range(capacity)]
    return jnp.concatenate(parts, axis=0)


def pick_kernel(capacity, here_ref, asked_ref, hot_ref, cold_ref, out_ref):
    devices = asked_ref.shape[0]
    hot_count, width = hot_ref.shape
    cold_count, cold_width = cold_ref.shape
    asked = asked_ref[...].reshape(devices, LANES)
    hot = dot(asked_select(asked, capacity, 0, hot_count), hot_ref[...])
    cold = dot(asked_select(asked, capacity, hot_count, cold_count), cold_ref[...])
    tiles = [hot[:, n * LANES : (n + 1) * LANES] for n in range(width // LANES)]
    for n in range(cold_width // LANES):
        tiles[n] = tiles[n] + cold[:, n * LANES : (n + 1) * LANES]
    stack = jnp.concatenate(tiles, axis=0).reshape(len(tiles) * capacity, devices, LANES)
    out_ref[...] = jnp.swapaxes(stack, 0, 1).reshape(out_ref.shape).astype(low)


def embed_kernel(capacity, hot_count, *refs):
    _, owner_ref, rank_ref, slot_ref, rows_ref, cold_ref = refs[:6]
    vector_ref, embedded_ref, normed_ref = refs[6:]
    tokens, width = embedded_ref.shape
    cold_width = cold_ref.shape[0]
    tiles = width // LANES
    base = owner_ref[...] * (tiles * capacity) + rank_ref[...]
    index = lax.broadcasted_iota(jnp.int32, (tokens, rows_ref.shape[0]), 1)
    parts = [
        dot(selected(index == base + n * capacity), rows_ref[...]) for n in range(tiles)
    ]
    vector = jnp.concatenate(parts, axis=1)
    narrow = vector[:, :cold_width].astype(low)
    vector_ref[...] = narrow
    embedded = jnp.where(slot_ref[...] >= hot_count, dot(narrow, cold_ref[...]), vector)
    embedded_ref[...] = embedded
    normed_ref[...] = layer_normalize(embedded)[0].astype(low)


def hidden_kernel(here_ref, normed_ref, weight_ref, hidden_ref, active_ref):
    hidden = dot(normed_ref[...], weight_ref[...])
    hidden_ref[...] = hidden
    active_ref[...] = silu(hidden).astype(low)


def forward_kernel(group, scale, head_size, *refs):
    here_ref, pieces = refs[0], refs[1 : 1 + group]
    weight_ref, active_ref, hidden_ref, mix_ref, cotangent_ref = refs[1 + group : 6 + group]
    gated_ref, delta_ref, gate_ref, early_ref, all_ref, normed_scr, mask_scr, att_scr = refs[6 + group :]
    tokens, width = cotangent_ref.shape
    order = arrival_order(group)
    here = here_ref[0]
    for n in range(1, group):
        normed_scr[n] = pieces[n][...]
    fill_mask(mask_scr, here, order, group, tokens, True)
    all_ref[0:tokens, :width] = active_ref[:, width : 2 * width]
    all_ref[0:tokens, width:] = active_ref[:, 3 * width :]

    def project(n, carry):
        hidden = dot(normed_scr[n], weight_ref[:, width : 2 * width])
        all_ref[tile(n, tokens), :width] = silu(hidden).astype(low)
        hidden = dot(normed_scr[n], weight_ref[:, 3 * width :])
        all_ref[tile(n, tokens), width:] = silu(hidden).astype(low)
        return carry

    lax.fori_loop(1, group, project, 0)
    masks = head_masks(tokens, head_size)

    def attend(n, carry):
        values = all_ref[:, tile(n)]
        queries = active_ref[:, tile(n + 2 * width // LANES)]
        keys = all_ref[:, tile(n + width // LANES)]
        parts = []
        for mask in masks:
            scores = dot(only(mask, queries), keys, (1, 1)) * scale
            weights = (silu(scores) * mask_scr[...]).astype(low)
            parts.append(dot(weights, values))
        att_scr[:, tile(n)] = merge(masks, parts)
        return carry

    lax.fori_loop(0, width // LANES, attend, 0, unroll=True)
    mixed, inverse_mix = layer_normalize(att_scr[...])
    gate = active_ref[:, :width].astype(f32)
    gated = (mixed * gate).astype(low)
    gated_ref[...] = gated
    delta_gated = dot(cotangent_ref[...], mix_ref[...], (1, 1))
    delta_ref[...] = normalize_back(delta_gated * gate, mixed, inverse_mix).astype(low)
    gate_hidden = (delta_gated * mixed * silu_slope(hidden_ref[:, :width])).astype(low)
    gate_ref[...] = gate_hidden
    share = width // group
    gated_t = gated.astype(f32).T.astype(low)
    hidden_t = gate_hidden.astype(f32).T.astype(low)
    for n in range(group):
        early_ref[n, 0:share] = gated_t[n * share : (n + 1) * share]
        early_ref[n, share : 2 * share] = hidden_t[n * share : (n + 1) * share]


def out_kernel(here_ref, gated_ref, mix_ref, embedded_ref, out_ref):
    out_ref[...] = (embedded_ref[...] + dot(gated_ref[...], mix_ref[...])).astype(low)


def query_kernel(group, scale, head_size, *refs):
    here_ref, pieces = refs[0], refs[1 : 1 + group]
    weight_ref, active_ref, all_ref, delta_ref, hidden_ref = refs[1 + group : 6 + group]
    out_ref, queries_ref, normed_scr, mask_scr = refs[6 + group :]
    tokens, width = delta_ref.shape
    for n in range(1, group):
        normed_scr[n] = pieces[n][...]
    queries_ref[0:tokens, :] = active_ref[:, 2 * width : 3 * width]

    def project(n, carry):
        hidden = dot(normed_scr[n], weight_ref[:, 2 * width : 3 * width])
        queries_ref[tile(n, tokens), :] = silu(hidden).astype(low)
        return carry

    lax.fori_loop(1, group, project, 0)
    fill_mask(mask_scr, here_ref[0], arrival_order(group), group, tokens, True)
    masks = head_masks(tokens, head_size)

    def step(n, carry):
        values = all_ref[:, tile(n)]
        queries = active_ref[:, tile(n + 2 * width // LANES)]
        keys = all_ref[:, tile(n + width // LANES)]
        delta = delta_ref[:, tile(n)]
        parts = []
        for mask in masks:
            scores = dot(only(mask, queries), keys, (1, 1)) * scale
            change = dot(only(mask, delta), values, (1, 1))
            change = (change * silu_slope(scores) * (mask_scr[...] * scale)).astype(low)
            parts.append(dot(change, keys))
        slope = silu_slope(hidden_ref[:, tile(n + 2 * width // LANES)])
        out_ref[:, tile(n)] = (merge(masks, parts) * slope).astype(low)
        return carry

    lax.fori_loop(0, width // LANES, step, 0, unroll=True)


def key_kernel(group, scale, head_size, *refs):
    here_ref, pieces = refs[0], refs[1 : 1 + group]
    active_ref, queries_ref, hidden_ref, query_ref, early_ref = refs[1 + group : 6 + group]
    rest_ref, columns = refs[6 + group], refs[7 + group : 7 + 2 * group]
    column_scr, delta_scr, mask_scr = refs[7 + 2 * group :]
    tokens, width = query_ref.shape
    for n in range(group):
        delta_scr[n * tokens : (n + 1) * tokens, :] = pieces[n][...]
    fill_mask(mask_scr, here_ref[0], arrival_order(group), group, tokens, False)
    masks = head_masks(tokens, head_size)
    tiles = width // LANES

    def step(n, carry):
        values = active_ref[:, tile(n + tiles)]
        queries = queries_ref[:, tile(n)]
        keys = active_ref[:, tile(n + 3 * tiles)]
        delta = delta_scr[:, tile(n)]
        value_parts, key_parts = [], []
        for mask in masks:
            scores = dot(only(mask, keys), queries, (1, 1)) * scale
            change = dot(only(mask, values), delta, (1, 1))
            sigmoid_v = sigmoid(scores)
            weights = (scores * sigmoid_v * mask_scr[...]).astype(low)
            slope = sigmoid_v * (1.0 + scores * (1.0 - sigmoid_v))
            change = (change * slope * (mask_scr[...] * scale)).astype(low)
            value_parts.append(dot(weights, delta))
            key_parts.append(dot(change, queries))
        for parts, at in ((value_parts, 0), (key_parts, 2)):
            slope = silu_slope(hidden_ref[:, tile(n + (at + 1) * tiles)])
            rest_ref[:, tile(n + at * tiles)] = (merge(masks, parts) * slope).astype(low)
        return carry

    lax.fori_loop(0, tiles, step, 0, unroll=True)
    rest_ref[:, width : 2 * width] = query_ref[...]
    late = rest_ref[...].astype(f32).T.astype(low)
    share = width // group
    for n in range(group):
        column_scr[n, : 2 * share] = early_ref[n]
        column_scr[n, 2 * share :] = late[3 * n * share : 3 * (n + 1) * share]
    for n, step in enumerate(arrival_order(group)):
        columns[n][...] = column_scr[target_of(here_ref[0], step, group)]


def row_kernel(head_rows, capacity, stride, *refs):
    _, gate_ref, rest_ref, weight_ref, embedded_ref, cotangent_ref = refs[:6]
    vector_ref, owner_ref, rank_ref, slot_ref, cold_ref, sent_ref = refs[6:]
    _, width = embedded_ref.shape
    cold_width = cold_ref.shape[0]
    tiles = width // LANES
    devices = sent_ref.shape[0] // (tiles * stride)
    delta_normed = dot(gate_ref[...], weight_ref[:, :width], (1, 1))
    delta_normed += dot(rest_ref[...], weight_ref[:, width:], (1, 1))
    normed, inverse = layer_normalize(embedded_ref[...])
    delta_embed = normalize_back(delta_normed, normed, inverse) + cotangent_ref[...].astype(f32)
    delta_low = delta_embed.astype(low)
    cold = slot_ref[...] >= head_rows
    cold_event = dot(delta_low, cold_ref[...], (1, 1))
    hot_event = jnp.where(cold, 0.0, delta_embed)
    narrow = jnp.where(cold, cold_event, hot_event[:, :cold_width])
    event = jnp.concatenate([narrow, hot_event[:, cold_width:]], axis=1).astype(low)
    cold_rows = jnp.where(cold, vector_ref[...].astype(f32), 0.0).astype(low)
    part = dot(cold_rows, delta_low, (0, 0)).astype(low)
    each = cold_width // devices
    row = lax.broadcasted_iota(jnp.int32, (1, cold_width), 1)
    own = (row // each) * (tiles * stride) + capacity + row % each
    place = as_row(owner_ref[...] * (tiles * stride) + rank_ref[...])
    place = jnp.concatenate([place, own], axis=1)
    both = jnp.concatenate([event, part], axis=0)
    index = lax.broadcasted_iota(jnp.int32, (sent_ref.shape[0], place.shape[1]), 0)
    total = None
    for n in range(tiles):
        chosen = selected(index == place + n * stride)
        term = dot(chosen, both[:, n * LANES : (n + 1) * LANES])
        total = term if n == 0 else total + term
    sent_ref[...] = total.astype(low)


def weight_kernel(group, count, *refs):
    here_ref, moved = refs[0], refs[1 : 1 + group]
    cotangents, normeds = refs[1 + group : 1 + 2 * group], refs[1 + 2 * group : 1 + 3 * group]
    own_ref = refs[1 + 3 * group]
    sends = refs[2 + 3 * group : 1 + 3 * group + count]
    part_scr = refs[1 + 3 * group + count]
    outer = here_ref[1]
    share = moved[0].shape[0] // 5
    chunk = own_ref.shape[0]
    top = bottom = None
    for n in range(group):
        first = dot(moved[n][:share], cotangents[n][...])
        second = dot(moved[n][share:], normeds[n][...])
        top = first if n == 0 else top + first
        bottom = second if n == 0 else bottom + second
    total = jnp.concatenate([top, bottom], axis=0)
    for n in range(count):
        part_scr[n] = total[n * chunk : (n + 1) * chunk]
    own_ref[...] = part_scr[outer]
    for step in range(1, count):
        sends[step - 1][...] = part_scr[target_of(outer, step, count)].astype(low)


def final_kernel(group, count, norm_scale, *refs):
    here_ref, pieces = refs[0], refs[1 : 1 + group]
    joined_ref, output_ref, piece_scr = refs[1 + group :]
    here, outer = here_ref[0], here_ref[1]
    width = output_ref.shape[0]
    chunk = piece_scr.shape[2]
    for n, step in enumerate(arrival_order(group)):
        source = source_of(here, step, group)
        for m in range(count):
            part = pieces[n][m * chunk : (m + 1) * chunk]
            piece_scr[source, source_of(outer, m, count)] = part
    share = width // group
    row = lax.broadcasted_iota(jnp.int32, (width, width), 0)
    column = lax.broadcasted_iota(jnp.int32, (width, width), 1)
    unit = (row == column).astype(f32).astype(low)
    blocks = [piece_scr[n].reshape(5 * share, width) for n in range(group)]
    for n in range(group):
        output_ref[n * share : (n + 1) * share, :] = blocks[n][:share].astype(f32) * norm_scale
    gate = jnp.concatenate([block[share : 2 * share] for block in blocks], axis=0)
    joined_ref[:, :width] = dot(unit, gate, (1, 1)) * norm_scale
    rest = jnp.concatenate([block[2 * share :] for block in blocks], axis=0)
    for n in range(3):
        columns = dot(unit, rest[n * width : (n + 1) * width], (1, 1)) * norm_scale
        joined_ref[:, (n + 1) * width : (n + 2) * width] = columns


def mine_kernel(capacity, stride, here_ref, arrived_ref, mine_ref):
    devices, each, width = mine_ref.shape
    total = arrived_ref[0].astype(f32)
    for n in range(1, devices):
        total = total + arrived_ref[n].astype(f32)
    first = range(capacity, (width // LANES) * stride, stride)
    sums = jnp.concatenate([total[n : n + each] for n in first], axis=1)
    mine_ref[...] = jnp.broadcast_to(sums[None], mine_ref.shape).astype(low)


def scatter_kernel(capacity, stride, here_ref, asked_ref, arrived_ref, hot_ref, cold_ref):
    devices = asked_ref.shape[0]
    hot_count, width = hot_ref.shape
    cold_count, cold_width = cold_ref.shape
    tiles = width // LANES
    asked = asked_ref[...].reshape(devices, LANES)
    stack = arrived_ref[...].astype(f32).reshape(devices, tiles * stride, LANES)
    stack = jnp.swapaxes(stack, 0, 1)
    rows = []
    for n in range(tiles):
        part = stack[n * stride : n * stride + capacity]
        rows.append(part.reshape(capacity * devices, LANES).astype(low))
    rows = jnp.concatenate(rows, axis=1)
    hot_ref[...] = dot(asked_select(asked, capacity, 0, hot_count), rows, (0, 0))
    chosen = asked_select(asked, capacity, hot_count, cold_count)
    cold_ref[...] = dot(chosen, rows[:, :cold_width], (0, 0))


def assemble(position, pieces, norm_scale, width):
    group, count = lax.axis_size("cp"), lax.axis_size("dp")
    share = width // group
    size = 5 * share // count
    if size % 16 == 0:
        return call(
            functools.partial(final_kernel, group, count, norm_scale),
            [position] + pieces,
            [shaped((width, 4 * width), f32), shaped((width, width), f32)],
            [pltpu.VMEM((group, count, size, width), low)],
        )
    result = jnp.zeros((group, count, size, width), low)
    for step, piece in zip(arrival_order(group), pieces):
        piece = piece.reshape(count, size, width)
        source = source_of(position[0], step, group)
        for n in range(count):
            place = (source, source_of(position[1], n, count), 0, 0)
            result = lax.dynamic_update_slice(result, piece[n][None, None], place)
    whole = result.reshape(group, count * size, width).astype(f32) * norm_scale
    output = whole[:, :share].reshape(width, width)
    gate = whole[:, share : 2 * share].reshape(width, width)
    rest = whole[:, 2 * share :].reshape(3 * width, width)
    return jnp.concatenate([gate, rest], axis=0).T, output


def local(
    row_owner,
    slot_row,
    hot_table,
    cold_table,
    cold_projection,
    joined_weight,
    output_weight,
    cotangent,
):
    tokens = slot_row.shape[0]
    width = output_weight.shape[0]
    hot_count = hot_table.shape[0]
    cold_count, cold_width = cold_table.shape
    head_size = width // HEADS
    score_scale = 1.0 / math.sqrt(head_size)
    everyone = ("dp", "cp")
    devices = lax.axis_size(everyone)
    group = lax.axis_size("cp")
    length = group * tokens
    position = jnp.stack([lax.axis_index("cp"), lax.axis_index("dp")]).astype(jnp.int32)
    capacity = 2 * tokens // devices + 2
    tiles = width // LANES
    each = cold_width // devices
    stride = capacity + each
    while tiles * stride % 8:
        stride += 1
    requests, rank, slot, owners = call(
        request_kernel,
        [position, row_owner.reshape(1, tokens), slot_row[None, :]],
        [
            shaped((devices, 1, LANES), jnp.int32),
            shaped((tokens, 1), jnp.int32),
            shaped((tokens, 1), jnp.int32),
            shaped((tokens, 1), jnp.int32),
        ],
    )
    asked = lax.all_to_all(requests, everyone, split_axis=0, concat_axis=0, tiled=True)
    cotangents = gather_pieces(cotangent, "cp")
    picked = call(
        functools.partial(pick_kernel, capacity),
        [position, asked, hot_table, cold_table],
        [shaped((devices * tiles * capacity, LANES), low)],
        limit=56,
    )[0]
    picked = picked.reshape(devices, tiles * capacity, LANES)
    rows_back = lax.all_to_all(picked, everyone, split_axis=0, concat_axis=0, tiled=True)
    rows_back = rows_back.reshape(devices * tiles * capacity, LANES)
    vector, embedded, normed_low = call(
        functools.partial(embed_kernel, capacity, hot_count),
        [position, owners, rank, slot, rows_back, cold_projection],
        [
            shaped((tokens, cold_width), low),
            shaped((tokens, width), f32),
            shaped((tokens, width), low),
        ],
    )
    normed_low, *cotangents = lax.optimization_barrier((normed_low, *cotangents))
    hidden, active = call(
        hidden_kernel,
        [position, normed_low, joined_weight],
        [shaped((tokens, 4 * width), f32), shaped((tokens, 4 * width), low)],
        flops=8 * tokens * width * width,
    )
    normeds = gather_pieces(normed_low, "cp")
    share = width // group
    work = 2 * tokens * length * width
    mask = pltpu.VMEM((tokens, length), f32)
    gated, delta_attended, gate_hidden, early, everything = call(
        functools.partial(forward_kernel, group, score_scale, head_size),
        [position, *normeds, joined_weight, active, hidden, output_weight, cotangent],
        [
            shaped((tokens, width), low),
            shaped((tokens, width), low),
            shaped((tokens, width), low),
            shaped((group, 2 * share, tokens), low),
            shaped((length, 2 * width), low),
        ],
        [pltpu.VMEM((group, tokens, width), low), mask, pltpu.VMEM((tokens, width), f32)],
        2 * work + 4 * length * width * width,
    )
    query_hidden, all_queries = call(
        functools.partial(query_kernel, group, score_scale, head_size),
        [position, *normeds, joined_weight, active, everything, delta_attended, hidden],
        [shaped((tokens, width), low), shaped((length, width), low)],
        [pltpu.VMEM((group, tokens, width), low), mask],
        3 * work,
    )
    deltas = gather_pieces(delta_attended, "cp")
    rest_hidden, *columns = call(
        functools.partial(key_kernel, group, score_scale, head_size),
        [position, *deltas, active, all_queries, hidden, query_hidden, early],
        [shaped((tokens, 3 * width), low)] + [shaped((5 * share, tokens), low)] * group,
        [pltpu.VMEM((group, 5 * share, tokens), low), pltpu.VMEM((length, width), low), mask],
        4 * work,
    )
    moved = columns[:1]
    for step, block in zip(arrival_order(group)[1:], columns[1:]):
        moved.append(exchange(block, "cp", step))
    sent = call(
        functools.partial(row_kernel, hot_count, capacity, stride),
        [
            position,
            gate_hidden,
            rest_hidden,
            joined_weight,
            embedded,
            cotangent,
            vector,
            owners,
            rank,
            slot,
            cold_projection,
        ],
        [shaped((devices * tiles * stride, LANES), low)],
        flops=8 * tokens * width * width,
        limit=56,
    )[0]
    sent = sent.reshape(devices, tiles * stride, LANES)
    arrived = lax.all_to_all(sent, everyone, split_axis=0, concat_axis=0, tiled=True)
    layer_out = call(
        out_kernel,
        [position, gated, output_weight, embedded],
        [shaped((tokens, width), low)],
        limit=56,
    )[0]
    count = lax.axis_size("dp")
    chunk = 5 * share // count
    own, *sends = call(
        functools.partial(weight_kernel, group, count),
        [position, *moved, *cotangents, *normeds],
        [shaped((chunk, width), f32)] + [shaped((chunk, width), low)] * (count - 1),
        [pltpu.VMEM((count, chunk, width), f32)],
        10 * share * length * width,
        limit=56,
    )
    for step, block in enumerate(sends, start=1):
        block = exchange(block, "dp", step)
        own = own + block.astype(f32)
    mine = own.astype(low)
    line = [mine]
    for step in range(1, count):
        line.append(exchange(mine, "dp", step))
    line = jnp.concatenate(line, axis=0)
    copies = call(
        functools.partial(mine_kernel, capacity, stride),
        [position, arrived],
        [shaped((devices, each, width), low)],
    )[0]
    projection = lax.all_to_all(copies, everyone, split_axis=0, concat_axis=0, tiled=True)
    hot_gradient, cold_gradient = call(
        functools.partial(scatter_kernel, capacity, stride),
        [position, asked, arrived.reshape(devices * tiles * stride, LANES)],
        [shaped((hot_count, width), f32), shaped((cold_count, cold_width), f32)],
        flops=4 * devices * capacity * hot_count * width,
        limit=56,
    )
    pieces = gather_pieces(line, "cp", (projection, hot_gradient, cold_gradient))
    norm_scale = (tokens * devices) ** (-0.5)
    joined_gradient, output_gradient = assemble(position, pieces, norm_scale, width)
    return (
        layer_out,
        hot_gradient,
        cold_gradient,
        projection.reshape(cold_width, width).astype(f32) * norm_scale,
        joined_gradient,
        output_gradient,
    )


def solution(mesh):
    placed = (
        P(("dp", "cp"), None),
        P(("dp", "cp")),
        P(("dp", "cp"), None),
        P(("dp", "cp"), None),
        P(),
        P(),
        P(),
        P(("dp", "cp"), None),
    )
    return jax.shard_map(
        local,
        mesh=mesh,
        in_specs=placed,
        out_specs=(
            P(("dp", "cp"), None),
            P(("dp", "cp"), None),
            P(("dp", "cp"), None),
            P(),
            P(),
            P(),
        ),
        check_vma=False,
    )
```

```python
import functools
import math

import jax
import jax.numpy as jnp
from jax import lax
from jax.experimental import pallas as pl
from jax.experimental.pallas import tpu as pltpu
from jax.sharding import PartitionSpec as P


HEADS = 8
LANES = 128


EPSILON = 1e-05
low = jnp.bfloat16
f32 = jnp.float32
SMEM = pl.BlockSpec(memory_space=pltpu.SMEM)
VMEM = pl.BlockSpec(memory_space=pltpu.VMEM)


def sigmoid(values):
    return 0.5 + 0.5 * jnp.tanh(0.5 * values)


def silu(values):
    return values * sigmoid(values)


def silu_slope(values):
    sigmoid_v = sigmoid(values)
    return sigmoid_v * (1.0 + values * (1.0 - sigmoid_v))


def layer_normalize(values):
    average = jnp.mean(values, axis=-1, keepdims=True)
    centred = values - average
    inverse = lax.rsqrt(jnp.mean(centred * centred, axis=-1, keepdims=True) + EPSILON)
    return (centred * inverse, inverse)


def normalize_back(gradient, normed, inverse):
    first_term = jnp.mean(gradient, axis=-1, keepdims=True)
    second_term = jnp.mean(gradient * normed, axis=-1, keepdims=True)
    return (gradient - first_term - normed * second_term) * inverse


def dot(left, right, contract=(1, 0)):
    dims = (((contract[0],), (contract[1],)), ((), ()))
    return lax.dot_general(left, right, dims, preferred_element_type=f32)


def power_of_two(count):
    return count & (count - 1) == 0


def source_of(here, step, count):
    if power_of_two(count):
        return here ^ step
    return (here + count - step) % count


def target_of(here, step, count):
    if power_of_two(count):
        return here ^ step
    return (here + step) % count


def exchange(block, axis, step):
    count = lax.axis_size(axis)
    pairs = [(i, target_of(i, step, count)) for i in range(count)]
    return lax.ppermute(block, axis, pairs)


def arrival_order(count):
    if not power_of_two(count) or count < 4:
        return list(range(count))
    return list(range(0, count, 2)) + list(range(1, count, 2))


def gather_pieces(block, axis, after=None):
    count = lax.axis_size(axis)
    if not power_of_two(count) or count < 4:
        return [block] + [exchange(block, axis, step) for step in range(1, count)]
    near = [block]
    for step in range(2, count, 2):
        near.append(exchange(block, axis, step))
    if after is not None:
        held = lax.optimization_barrier((*near[1:], *after))
        near = [block, *held[: len(near) - 1]]
    return near + [exchange(piece, axis, 1) for piece in near]


def call(kernel, operands, outs, scratch=(), flops=0, scalars=1, limit=24, place=VMEM):
    moved = sum(x.size * x.dtype.itemsize for x in list(operands) + list(outs))
    return pl.pallas_call(
        kernel,
        out_shape=outs,
        in_specs=[SMEM] * scalars + [VMEM] * (len(operands) - scalars),
        out_specs=[place] * len(outs),
        scratch_shapes=list(scratch),
        cost_estimate=pl.CostEstimate(flops=flops, bytes_accessed=moved, transcendentals=0),
        compiler_params=pltpu.CompilerParams(vmem_limit_bytes=limit << 20),
    )(*operands)


def shaped(shape, dtype):
    return jax.ShapeDtypeStruct(shape, dtype)


def tile(index, size=LANES):
    return pl.ds(pl.multiple_of(index * size, size), size)


def head_masks(rows, head_size):
    lane = lax.broadcasted_iota(jnp.int32, (rows, LANES), 1)
    return [lane // head_size == n for n in range(LANES // head_size)]


def only(mask, values):
    return jnp.where(mask, values, jnp.zeros((), values.dtype))


def merge(masks, parts):
    result = parts[-1]
    for mask, part in zip(masks[:-1], parts[:-1]):
        result = jnp.where(mask, part, result)
    return result


def fill_mask(mask_ref, here, order, group, tokens, forward):
    row = lax.broadcasted_iota(jnp.int32, (tokens, tokens), 0)
    column = lax.broadcasted_iota(jnp.int32, (tokens, tokens), 1)
    for n, step in enumerate(order):
        gap = (here - source_of(here, step, group)) * tokens
        allowed = (column - row <= gap) if forward else (column - row >= gap)
        mask_ref[:, n * tokens : (n + 1) * tokens] = allowed.astype(f32)


def unit_mask(size):
    row = lax.broadcasted_iota(jnp.int32, (size, size), 0)
    return row == lax.broadcasted_iota(jnp.int32, (size, size), 1)


def as_row(column):
    return jnp.sum(jnp.where(unit_mask(column.shape[0]), column, 0), axis=0, keepdims=True)


def as_column(row):
    return jnp.sum(jnp.where(unit_mask(row.shape[1]), row, 0), axis=1, keepdims=True)


def selected(flags):
    return flags.astype(f32).astype(low)


def request_kernel(here_ref, owner_ref, slot_ref, request_ref, rank_ref, column_ref, owners_ref):
    tokens = owner_ref.shape[1]
    devices = request_ref.shape[0]
    owners = as_column(owner_ref[...])
    owners_ref[...] = owners
    named = owners == lax.broadcasted_iota(jnp.int32, (tokens, devices), 1)
    row = lax.broadcasted_iota(jnp.int32, (tokens, tokens), 0)
    lower = selected(row > lax.broadcasted_iota(jnp.int32, (tokens, tokens), 1))
    earlier = dot(lower, selected(named))
    rank = jnp.sum(jnp.where(named, earlier, 0.0), axis=1, keepdims=True).astype(jnp.int32)
    rank_ref[...] = rank
    slot = as_column(slot_ref[...])
    column_ref[...] = slot
    ranked = rank == lax.broadcasted_iota(jnp.int32, (tokens, LANES), 1)
    code = slot + 1
    high = jnp.where(ranked, code >> 6, 0).astype(f32).astype(low)
    rest = jnp.where(ranked, code & 63, 0).astype(f32).astype(low)
    names = selected(named)
    total = dot(names, high, (0, 0)) * 64.0 + dot(names, rest, (0, 0)) - 1.0
    request_ref[...] = total.astype(jnp.int32).reshape(devices, 1, LANES)


def asked_select(asked, capacity, first, count):
    index = lax.broadcasted_iota(jnp.int32, (asked.shape[0], count), 1) + first
    parts = [selected(asked[:, n : n + 1] == index) for n in range(capacity)]
    return jnp.concatenate(parts, axis=0)


def pick_kernel(capacity, here_ref, asked_ref, hot_ref, cold_ref, out_ref):
    devices = asked_ref.shape[0]
    hot_count, width = hot_ref.shape
    cold_count, cold_width = cold_ref.shape
    asked = asked_ref[...].reshape(devices, LANES)
    hot = dot(asked_select(asked, capacity, 0, hot_count), hot_ref[...])
    cold = dot(asked_select(asked, capacity, hot_count, cold_count), cold_ref[...])
    tiles = [hot[:, n * LANES : (n + 1) * LANES] for n in range(width // LANES)]
    for n in range(cold_width // LANES):
        tiles[n] = tiles[n] + cold[:, n * LANES : (n + 1) * LANES]
    stack = jnp.concatenate(tiles, axis=0).reshape(len(tiles) * capacity, devices, LANES)
    out_ref[...] = jnp.swapaxes(stack, 0, 1).reshape(out_ref.shape).astype(low)


def embed_kernel(capacity, hot_count, *refs):
    _, owner_ref, rank_ref, slot_ref, rows_ref, cold_ref = refs[:6]
    vector_ref, embedded_ref, normed_ref = refs[6:]
    tokens, width = embedded_ref.shape
    cold_width = cold_ref.shape[0]
    tiles = width // LANES
    base = owner_ref[...] * (tiles * capacity) + rank_ref[...]
    index = lax.broadcasted_iota(jnp.int32, (tokens, rows_ref.shape[0]), 1)
    parts = [
        dot(selected(index == base + n * capacity), rows_ref[...]) for n in range(tiles)
    ]
    vector = jnp.concatenate(parts, axis=1)
    narrow = vector[:, :cold_width].astype(low)
    vector_ref[...] = narrow
    embedded = jnp.where(slot_ref[...] >= hot_count, dot(narrow, cold_ref[...]), vector)
    embedded_ref[...] = embedded
    normed_ref[...] = layer_normalize(embedded)[0].astype(low)


def hidden_kernel(here_ref, normed_ref, weight_ref, hidden_ref, active_ref):
    hidden = dot(normed_ref[...], weight_ref[...])
    hidden_ref[...] = hidden
    active_ref[...] = silu(hidden).astype(low)


def forward_kernel(group, scale, head_size, *refs):
    here_ref, pieces = refs[0], refs[1 : 1 + group]
    weight_ref, active_ref, hidden_ref, mix_ref, cotangent_ref = refs[1 + group : 6 + group]
    gated_ref, delta_ref, gate_ref, early_ref, all_ref, normed_scr, mask_scr, att_scr = refs[6 + group :]
    tokens, width = cotangent_ref.shape
    order = arrival_order(group)
    here = here_ref[0]
    for n in range(1, group):
        normed_scr[n] = pieces[n][...]
    fill_mask(mask_scr, here, order, group, tokens, True)
    all_ref[0:tokens, :width] = active_ref[:, width : 2 * width]
    all_ref[0:tokens, width:] = active_ref[:, 3 * width :]

    def project(n, carry):
        hidden = dot(normed_scr[n], weight_ref[:, width : 2 * width])
        all_ref[tile(n, tokens), :width] = silu(hidden).astype(low)
        hidden = dot(normed_scr[n], weight_ref[:, 3 * width :])
        all_ref[tile(n, tokens), width:] = silu(hidden).astype(low)
        return carry

    lax.fori_loop(1, group, project, 0)
    masks = head_masks(tokens, head_size)

    def attend(n, carry):
        values = all_ref[:, tile(n)]
        queries = active_ref[:, tile(n + 2 * width // LANES)]
        keys = all_ref[:, tile(n + width // LANES)]
        parts = []
        for mask in masks:
            scores = dot(only(mask, queries), keys, (1, 1)) * scale
            weights = (silu(scores) * mask_scr[...]).astype(low)
            parts.append(dot(weights, values))
        att_scr[:, tile(n)] = merge(masks, parts)
        return carry

    lax.fori_loop(0, width // LANES, attend, 0, unroll=True)
    mixed, inverse_mix = layer_normalize(att_scr[...])
    gate = active_ref[:, :width].astype(f32)
    gated = (mixed * gate).astype(low)
    gated_ref[...] = gated
    delta_gated = dot(cotangent_ref[...], mix_ref[...], (1, 1))
    delta_ref[...] = normalize_back(delta_gated * gate, mixed, inverse_mix).astype(low)
    gate_hidden = (delta_gated * mixed * silu_slope(hidden_ref[:, :width])).astype(low)
    gate_ref[...] = gate_hidden
    share = width // group
    gated_t = gated.astype(f32).T.astype(low)
    hidden_t = gate_hidden.astype(f32).T.astype(low)
    for n in range(group):
        early_ref[n, 0:share] = gated_t[n * share : (n + 1) * share]
        early_ref[n, share : 2 * share] = hidden_t[n * share : (n + 1) * share]


def out_kernel(here_ref, gated_ref, mix_ref, embedded_ref, out_ref):
    out_ref[...] = (embedded_ref[...] + dot(gated_ref[...], mix_ref[...])).astype(low)


def query_kernel(group, scale, head_size, *refs):
    here_ref, pieces = refs[0], refs[1 : 1 + group]
    weight_ref, active_ref, all_ref, delta_ref, hidden_ref = refs[1 + group : 6 + group]
    out_ref, queries_ref, normed_scr, mask_scr = refs[6 + group :]
    tokens, width = delta_ref.shape
    for n in range(1, group):
        normed_scr[n] = pieces[n][...]
    queries_ref[0:tokens, :] = active_ref[:, 2 * width : 3 * width]

    def project(n, carry):
        hidden = dot(normed_scr[n], weight_ref[:, 2 * width : 3 * width])
        queries_ref[tile(n, tokens), :] = silu(hidden).astype(low)
        return carry

    lax.fori_loop(1, group, project, 0)
    fill_mask(mask_scr, here_ref[0], arrival_order(group), group, tokens, True)
    masks = head_masks(tokens, head_size)

    def step(n, carry):
        values = all_ref[:, tile(n)]
        queries = active_ref[:, tile(n + 2 * width // LANES)]
        keys = all_ref[:, tile(n + width // LANES)]
        delta = delta_ref[:, tile(n)]
        parts = []
        for mask in masks:
            scores = dot(only(mask, queries), keys, (1, 1)) * scale
            change = dot(only(mask, delta), values, (1, 1))
            change = (change * silu_slope(scores) * (mask_scr[...] * scale)).astype(low)
            parts.append(dot(change, keys))
        slope = silu_slope(hidden_ref[:, tile(n + 2 * width // LANES)])
        out_ref[:, tile(n)] = (merge(masks, parts) * slope).astype(low)
        return carry

    lax.fori_loop(0, width // LANES, step, 0, unroll=True)


def key_kernel(group, scale, head_size, *refs):
    here_ref, pieces = refs[0], refs[1 : 1 + group]
    active_ref, queries_ref, hidden_ref, query_ref, early_ref = refs[1 + group : 6 + group]
    rest_ref, columns = refs[6 + group], refs[7 + group : 7 + 2 * group]
    column_scr, delta_scr, mask_scr = refs[7 + 2 * group :]
    tokens, width = query_ref.shape
    for n in range(group):
        delta_scr[n * tokens : (n + 1) * tokens, :] = pieces[n][...]
    fill_mask(mask_scr, here_ref[0], arrival_order(group), group, tokens, False)
    masks = head_masks(tokens, head_size)
    tiles = width // LANES

    def step(n, carry):
        values = active_ref[:, tile(n + tiles)]
        queries = queries_ref[:, tile(n)]
        keys = active_ref[:, tile(n + 3 * tiles)]
        delta = delta_scr[:, tile(n)]
        value_parts, key_parts = [], []
        for mask in masks:
            scores = dot(only(mask, keys), queries, (1, 1)) * scale
            change = dot(only(mask, values), delta, (1, 1))
            sigmoid_v = sigmoid(scores)
            weights = (scores * sigmoid_v * mask_scr[...]).astype(low)
            slope = sigmoid_v * (1.0 + scores * (1.0 - sigmoid_v))
            change = (change * slope * (mask_scr[...] * scale)).astype(low)
            value_parts.append(dot(weights, delta))
            key_parts.append(dot(change, queries))
        for parts, at in ((value_parts, 0), (key_parts, 2)):
            slope = silu_slope(hidden_ref[:, tile(n + (at + 1) * tiles)])
            rest_ref[:, tile(n + at * tiles)] = (merge(masks, parts) * slope).astype(low)
        return carry

    lax.fori_loop(0, tiles, step, 0, unroll=True)
    rest_ref[:, width : 2 * width] = query_ref[...]
    late = rest_ref[...].astype(f32).T.astype(low)
    share = width // group
    for n in range(group):
        column_scr[n, : 2 * share] = early_ref[n]
        column_scr[n, 2 * share :] = late[3 * n * share : 3 * (n + 1) * share]
    for n, step in enumerate(arrival_order(group)):
        columns[n][...] = column_scr[target_of(here_ref[0], step, group)]


def row_kernel(head_rows, capacity, stride, *refs):
    _, gate_ref, rest_ref, weight_ref, embedded_ref, cotangent_ref = refs[:6]
    vector_ref, owner_ref, rank_ref, slot_ref, cold_ref, sent_ref = refs[6:]
    _, width = embedded_ref.shape
    cold_width = cold_ref.shape[0]
    tiles = width // LANES
    devices = sent_ref.shape[0] // (tiles * stride)
    delta_normed = dot(gate_ref[...], weight_ref[:, :width], (1, 1))
    delta_normed += dot(rest_ref[...], weight_ref[:, width:], (1, 1))
    normed, inverse = layer_normalize(embedded_ref[...])
    delta_embed = normalize_back(delta_normed, normed, inverse) + cotangent_ref[...].astype(f32)
    delta_low = delta_embed.astype(low)
    cold = slot_ref[...] >= head_rows
    cold_event = dot(delta_low, cold_ref[...], (1, 1))
    hot_event = jnp.where(cold, 0.0, delta_embed)
    narrow = jnp.where(cold, cold_event, hot_event[:, :cold_width])
    event = jnp.concatenate([narrow, hot_event[:, cold_width:]], axis=1).astype(low)
    cold_rows = jnp.where(cold, vector_ref[...].astype(f32), 0.0).astype(low)
    part = dot(cold_rows, delta_low, (0, 0)).astype(low)
    each = cold_width // devices
    row = lax.broadcasted_iota(jnp.int32, (1, cold_width), 1)
    own = (row // each) * (tiles * stride) + capacity + row % each
    place = as_row(owner_ref[...] * (tiles * stride) + rank_ref[...])
    place = jnp.concatenate([place, own], axis=1)
    both = jnp.concatenate([event, part], axis=0)
    index = lax.broadcasted_iota(jnp.int32, (sent_ref.shape[0], place.shape[1]), 0)
    total = None
    for n in range(tiles):
        chosen = selected(index == place + n * stride)
        term = dot(chosen, both[:, n * LANES : (n + 1) * LANES])
        total = term if n == 0 else total + term
    sent_ref[...] = total.astype(low)


def weight_kernel(group, count, *refs):
    here_ref, moved = refs[0], refs[1 : 1 + group]
    cotangents, normeds = refs[1 + group : 1 + 2 * group], refs[1 + 2 * group : 1 + 3 * group]
    own_ref = refs[1 + 3 * group]
    sends = refs[2 + 3 * group : 1 + 3 * group + count]
    part_scr = refs[1 + 3 * group + count]
    outer = here_ref[1]
    share = moved[0].shape[0] // 5
    chunk = own_ref.shape[0]
    top = bottom = None
    for n in range(group):
        first = dot(moved[n][:share], cotangents[n][...])
        second = dot(moved[n][share:], normeds[n][...])
        top = first if n == 0 else top + first
        bottom = second if n == 0 else bottom + second
    total = jnp.concatenate([top, bottom], axis=0)
    for n in range(count):
        part_scr[n] = total[n * chunk : (n + 1) * chunk]
    own_ref[...] = part_scr[outer]
    for step in range(1, count):
        sends[step - 1][...] = part_scr[target_of(outer, step, count)].astype(low)


def final_kernel(group, count, norm_scale, *refs):
    here_ref, pieces = refs[0], refs[1 : 1 + group]
    joined_ref, output_ref, piece_scr, joined_scr, output_scr, done = refs[1 + group :]
    here, outer = here_ref[0], here_ref[1]
    width = output_ref.shape[0]
    chunk = piece_scr.shape[2]
    for n, step in enumerate(arrival_order(group)):
        source = source_of(here, step, group)
        for m in range(count):
            part = pieces[n][m * chunk : (m + 1) * chunk]
            piece_scr[source, source_of(outer, m, count)] = part
    share = width // group
    row = lax.broadcasted_iota(jnp.int32, (width, width), 0)
    column = lax.broadcasted_iota(jnp.int32, (width, width), 1)
    unit = (row == column).astype(f32).astype(low)
    blocks = [piece_scr[n].reshape(5 * share, width) for n in range(group)]
    for n in range(group):
        output_scr[n * share : (n + 1) * share, :] = blocks[n][:share].astype(f32) * norm_scale
    copies = [pltpu.make_async_copy(output_scr, output_ref, done.at[4])]
    copies[0].start()
    gate = jnp.concatenate([block[share : 2 * share] for block in blocks], axis=0)
    rest = jnp.concatenate([block[2 * share :] for block in blocks], axis=0)
    for n in range(4):
        rows = gate if n == 0 else rest[(n - 1) * width : n * width]
        joined_scr[n] = dot(unit, rows, (1, 1)) * norm_scale
        target = joined_ref.at[:, n * width : (n + 1) * width]
        copies.append(pltpu.make_async_copy(joined_scr.at[n], target, done.at[n]))
        copies[-1].start()
    for copy in copies:
        copy.wait()


def mine_kernel(capacity, stride, here_ref, arrived_ref, mine_ref):
    devices, each, width = mine_ref.shape
    total = arrived_ref[0].astype(f32)
    for n in range(1, devices):
        total = total + arrived_ref[n].astype(f32)
    first = range(capacity, (width // LANES) * stride, stride)
    sums = jnp.concatenate([total[n : n + each] for n in first], axis=1)
    mine_ref[...] = jnp.broadcast_to(sums[None], mine_ref.shape).astype(low)


def scatter_kernel(capacity, stride, here_ref, asked_ref, arrived_ref, hot_ref, cold_ref):
    devices = asked_ref.shape[0]
    hot_count, width = hot_ref.shape
    cold_count, cold_width = cold_ref.shape
    tiles = width // LANES
    asked = asked_ref[...].reshape(devices, LANES)
    stack = arrived_ref[...].astype(f32).reshape(devices, tiles * stride, LANES)
    stack = jnp.swapaxes(stack, 0, 1)
    rows = []
    for n in range(tiles):
        part = stack[n * stride : n * stride + capacity]
        rows.append(part.reshape(capacity * devices, LANES).astype(low))
    rows = jnp.concatenate(rows, axis=1)
    hot_ref[...] = dot(asked_select(asked, capacity, 0, hot_count), rows, (0, 0))
    chosen = asked_select(asked, capacity, hot_count, cold_count)
    cold_ref[...] = dot(chosen, rows[:, :cold_width], (0, 0))


def assemble(position, pieces, norm_scale, width):
    group, count = lax.axis_size("cp"), lax.axis_size("dp")
    share = width // group
    size = 5 * share // count
    if size % 16 == 0:
        return call(
            functools.partial(final_kernel, group, count, norm_scale),
            [position] + pieces,
            [shaped((width, 4 * width), f32), shaped((width, width), f32)],
            [
                pltpu.VMEM((group, count, size, width), low),
                pltpu.VMEM((4, width, width), f32),
                pltpu.VMEM((width, width), f32),
                pltpu.SemaphoreType.DMA((5,)),
            ],
            place=pl.BlockSpec(memory_space=pl.ANY),
        )
    result = jnp.zeros((group, count, size, width), low)
    for step, piece in zip(arrival_order(group), pieces):
        piece = piece.reshape(count, size, width)
        source = source_of(position[0], step, group)
        for n in range(count):
            place = (source, source_of(position[1], n, count), 0, 0)
            result = lax.dynamic_update_slice(result, piece[n][None, None], place)
    whole = result.reshape(group, count * size, width).astype(f32) * norm_scale
    output = whole[:, :share].reshape(width, width)
    gate = whole[:, share : 2 * share].reshape(width, width)
    rest = whole[:, 2 * share :].reshape(3 * width, width)
    return jnp.concatenate([gate, rest], axis=0).T, output


def local(
    row_owner,
    slot_row,
    hot_table,
    cold_table,
    cold_projection,
    joined_weight,
    output_weight,
    cotangent,
):
    tokens = slot_row.shape[0]
    width = output_weight.shape[0]
    hot_count = hot_table.shape[0]
    cold_count, cold_width = cold_table.shape
    head_size = width // HEADS
    score_scale = 1.0 / math.sqrt(head_size)
    everyone = ("dp", "cp")
    devices = lax.axis_size(everyone)
    group = lax.axis_size("cp")
    length = group * tokens
    position = jnp.stack([lax.axis_index("cp"), lax.axis_index("dp")]).astype(jnp.int32)
    capacity = 2 * tokens // devices + 2
    tiles = width // LANES
    each = cold_width // devices
    stride = capacity + each
    while tiles * stride % 8:
        stride += 1
    requests, rank, slot, owners = call(
        request_kernel,
        [position, row_owner.reshape(1, tokens), slot_row[None, :]],
        [
            shaped((devices, 1, LANES), jnp.int32),
            shaped((tokens, 1), jnp.int32),
            shaped((tokens, 1), jnp.int32),
            shaped((tokens, 1), jnp.int32),
        ],
    )
    asked = lax.all_to_all(requests, everyone, split_axis=0, concat_axis=0, tiled=True)
    cotangents = gather_pieces(cotangent, "cp")
    picked = call(
        functools.partial(pick_kernel, capacity),
        [position, asked, hot_table, cold_table],
        [shaped((devices * tiles * capacity, LANES), low)],
        limit=56,
    )[0]
    picked = picked.reshape(devices, tiles * capacity, LANES)
    rows_back = lax.all_to_all(picked, everyone, split_axis=0, concat_axis=0, tiled=True)
    rows_back = rows_back.reshape(devices * tiles * capacity, LANES)
    vector, embedded, normed_low = call(
        functools.partial(embed_kernel, capacity, hot_count),
        [position, owners, rank, slot, rows_back, cold_projection],
        [
            shaped((tokens, cold_width), low),
            shaped((tokens, width), f32),
            shaped((tokens, width), low),
        ],
    )
    normed_low, *cotangents = lax.optimization_barrier((normed_low, *cotangents))
    hidden, active = call(
        hidden_kernel,
        [position, normed_low, joined_weight],
        [shaped((tokens, 4 * width), f32), shaped((tokens, 4 * width), low)],
        flops=8 * tokens * width * width,
    )
    normeds = gather_pieces(normed_low, "cp")
    share = width // group
    work = 2 * tokens * length * width
    mask = pltpu.VMEM((tokens, length), f32)
    gated, delta_attended, gate_hidden, early, everything = call(
        functools.partial(forward_kernel, group, score_scale, head_size),
        [position, *normeds, joined_weight, active, hidden, output_weight, cotangent],
        [
            shaped((tokens, width), low),
            shaped((tokens, width), low),
            shaped((tokens, width), low),
            shaped((group, 2 * share, tokens), low),
            shaped((length, 2 * width), low),
        ],
        [pltpu.VMEM((group, tokens, width), low), mask, pltpu.VMEM((tokens, width), f32)],
        2 * work + 4 * length * width * width,
    )
    query_hidden, all_queries = call(
        functools.partial(query_kernel, group, score_scale, head_size),
        [position, *normeds, joined_weight, active, everything, delta_attended, hidden],
        [shaped((tokens, width), low), shaped((length, width), low)],
        [pltpu.VMEM((group, tokens, width), low), mask],
        3 * work,
    )
    deltas = gather_pieces(delta_attended, "cp")
    rest_hidden, *columns = call(
        functools.partial(key_kernel, group, score_scale, head_size),
        [position, *deltas, active, all_queries, hidden, query_hidden, early],
        [shaped((tokens, 3 * width), low)] + [shaped((5 * share, tokens), low)] * group,
        [pltpu.VMEM((group, 5 * share, tokens), low), pltpu.VMEM((length, width), low), mask],
        4 * work,
    )
    moved = columns[:1]
    for step, block in zip(arrival_order(group)[1:], columns[1:]):
        moved.append(exchange(block, "cp", step))
    sent = call(
        functools.partial(row_kernel, hot_count, capacity, stride),
        [
            position,
            gate_hidden,
            rest_hidden,
            joined_weight,
            embedded,
            cotangent,
            vector,
            owners,
            rank,
            slot,
            cold_projection,
        ],
        [shaped((devices * tiles * stride, LANES), low)],
        flops=8 * tokens * width * width,
        limit=56,
    )[0]
    sent = sent.reshape(devices, tiles * stride, LANES)
    arrived = lax.all_to_all(sent, everyone, split_axis=0, concat_axis=0, tiled=True)
    layer_out = call(
        out_kernel,
        [position, gated, output_weight, embedded],
        [shaped((tokens, width), low)],
        limit=56,
    )[0]
    count = lax.axis_size("dp")
    chunk = 5 * share // count
    own, *sends = call(
        functools.partial(weight_kernel, group, count),
        [position, *moved, *cotangents, *normeds],
        [shaped((chunk, width), f32)] + [shaped((chunk, width), low)] * (count - 1),
        [pltpu.VMEM((count, chunk, width), f32)],
        10 * share * length * width,
        limit=56,
    )
    for step, block in enumerate(sends, start=1):
        block = exchange(block, "dp", step)
        own = own + block.astype(f32)
    mine = own.astype(low)
    line = [mine]
    for step in range(1, count):
        line.append(exchange(mine, "dp", step))
    line = jnp.concatenate(line, axis=0)
    copies = call(
        functools.partial(mine_kernel, capacity, stride),
        [position, arrived],
        [shaped((devices, each, width), low)],
    )[0]
    projection = lax.all_to_all(copies, everyone, split_axis=0, concat_axis=0, tiled=True)
    hot_gradient, cold_gradient = call(
        functools.partial(scatter_kernel, capacity, stride),
        [position, asked, arrived.reshape(devices * tiles * stride, LANES)],
        [shaped((hot_count, width), f32), shaped((cold_count, cold_width), f32)],
        flops=4 * devices * capacity * hot_count * width,
        limit=56,
    )
    pieces = gather_pieces(line, "cp", (hot_gradient, cold_gradient))
    norm_scale = (tokens * devices) ** (-0.5)
    joined_gradient, output_gradient = assemble(position, pieces, norm_scale, width)
    return (
        layer_out,
        hot_gradient,
        cold_gradient,
        projection.reshape(cold_width, width).astype(f32) * norm_scale,
        joined_gradient,
        output_gradient,
    )


def solution(mesh):
    placed = (
        P(("dp", "cp"), None),
        P(("dp", "cp")),
        P(("dp", "cp"), None),
        P(("dp", "cp"), None),
        P(),
        P(),
        P(),
        P(("dp", "cp"), None),
    )
    return jax.shard_map(
        local,
        mesh=mesh,
        in_specs=placed,
        out_specs=(
            P(("dp", "cp"), None),
            P(("dp", "cp"), None),
            P(("dp", "cp"), None),
            P(),
            P(),
            P(),
        ),
        check_vma=False,
    )
```
